32 devices in a mesh: expert: 2 (over y), seq: 16 (over z, x, core).
Axes of the slice: x: 2, y: 2, z: 4, core: 2. Of those that a mesh axis runs over, the one named last changes fastest.
Arguments:
- acts: bfloat16 [2, 2048, 1024], P('expert', 'seq'), may hold values from -6 to 6
- queries: bfloat16 [2, 2048, 1024], P('expert', 'seq'), may hold values from -32 to 32
- keys: bfloat16 [2, 2048, 1024], P('expert', 'seq'), may hold values from -6 to 6
- values: bfloat16 [2, 2048, 1024], P('expert', 'seq'), may hold values from -6 to 6
- grad_out: bfloat16 [2, 2048, 1024], P('expert', 'seq'), may hold values from -6 to 6
- gain: float32 [1024], replicated, may hold values from 0.5 to 1.5
- router: bfloat16 [1024, 2], replicated, may hold values from -0.1875 to 0.1875
- w_in: bfloat16 [2, 2048, 1024], P('expert', 'seq'), may hold values from -0.1875 to 0.1875
- w_out: bfloat16 [2, 2048, 1024], P('expert', 'seq'), may hold values from -0.125 to 0.125
- routes: int32 [2, 2048, 1], P('expert', 'seq'), may hold values from 0 to 1; in each aligned block of 128 rows (0 to 127, 128 to 255, ..., all dimensions but the last counted through in order) at most 80 rows name the same one
- tissue: int32 [2, 4], P('expert'), may hold values 0 or 1
Outputs:
- grad_acts: bfloat16 [2, 2048, 1024], P('expert', 'seq')
- grad_queries: bfloat16 [2, 2048, 1024], P('expert', 'seq')
- grad_keys: bfloat16 [2, 2048, 1024], P('expert', 'seq')
- grad_values: bfloat16 [2, 2048, 1024], P('expert', 'seq')
- grad_router: float32 [1024, 2], replicated
- grad_gain: float32 [1024], replicated
The draws below stay inside these ranges and needn't reach their ends.
Inputs may be any that keep to these rules, and one draw needn't show every extreme that they name: `routes`: among the tiles of one run of 128 tiles of a slide, no expert is named more than 80 times, a bound that some block reaches.
All inputs are finite; a program needn't handle non-finite values. No bound on the sum of `tissue` on one device may be relied on, other than what follows from the above.
Results may differ from the reference program's by a relative error of at most 0.015.
Values may be sent and summed in bfloat16 or wider, within the bound.
A program may use at most 64 MiB of HBM per device.

```python
import math
import jax
import jax.numpy as jnp
import numpy as np
from jax import lax

D = 1024
HEADS = 16
HEAD = 64
FF = 2048
REACH = 128
BLOCK = 512
TOK_DEV = 128
SLIDES = 2
EXPERTS = 2
LEN = 2048
NBLOCKS = 4
CAP = 80
N_SEQ = 16


def key_field(key):
    return jnp.clip(jax.random.normal(jax.random.fold_in(key, 17), (SLIDES, LEN, D), jnp.float32), -6.0, 6.0)


def draw_keys(key, part):
    field = key_field(key)
    return field.astype(jnp.bfloat16)


def draw_queries(key, part):
    fresh = jnp.clip(jax.random.normal(jax.random.fold_in(key, 29), (SLIDES, LEN, D), jnp.float32), -6.0, 6.0)
    return fresh.astype(jnp.bfloat16)


def with_ends(array, rng, least, largest):
    spot = [jax.random.randint(jax.random.fold_in(rng, axis), (), 0, length) for axis, length in enumerate(array.shape)]
    widest = array.shape.index(max(array.shape))
    beside = spot[:widest] + [(spot[widest] + 1) % array.shape[widest]] + spot[widest + 1:]
    return array.at[tuple(spot)].set(least).at[tuple(beside)].set(largest)


def steps_of(key, dims, split, low, top_value):
    factor_of = 1.0
    for axis_at, shards_of in split:
        steps = jax.random.uniform(jax.random.fold_in(jax.random.fold_in(key, 6), axis_at), (shards_of,), jnp.float32, low / len(split), top_value / len(split))
        factor_of = factor_of * jnp.repeat(jnp.exp(steps), dims[axis_at] // shards_of).reshape((-1,) + (1,) * (len(dims) - 1 - axis_at))
    return factor_of


def routed_block(stream_key, own, number, rows, count, top, reach, lean):
    sequence = jax.random.permutation(stream_key, count)
    heavy_load, ordinary = load_shares(count, rows * top, reach, lean, True), load_shares(count, rows * top, reach, lean, False)
    places = jnp.arange(count)

    def named(tallies, offset_by):
        used = int((tallies > 0).sum())
        fixed = max(1, used // 4)
        passed = fixed + (places - fixed + offset_by * (used - fixed)) % max(1, count - fixed)
        return jnp.zeros((count,), jnp.int32).at[sequence[jnp.where(places < fixed, places, passed)]].set(jnp.asarray(tallies, jnp.int32))

    tallies = jnp.where(number % 4 == 0, named(heavy_load, number // 4), named(ordinary, number - number // 4 - 1))
    mixed = jax.random.permutation(jax.random.fold_in(own, 3), count)
    giver, receiver = mixed[0:count // 2 * 2:2], mixed[1:count // 2 * 2:2]
    slack = jnp.minimum(tallies[giver] - 1, reach - tallies[receiver]) // 2
    slack = jnp.where((giver == sequence[0]) | (receiver == sequence[0]) | (tallies[receiver] == 0), 0, jnp.maximum(slack, 0))
    passed = jax.random.randint(jax.random.fold_in(own, 4), (count // 2,), 0, 1 << 20) % (slack + 1)
    tallies = tallies.at[giver].add(-passed).at[receiver].add(passed)
    labels = jnp.searchsorted(jnp.cumsum(tallies), jnp.arange(rows * top), side="right").astype(jnp.int32)
    grid = labels.reshape(top, rows).T
    grid = grid[jax.random.permutation(jax.random.fold_in(own, 1), rows)]
    offset_by = jax.random.randint(jax.random.fold_in(own, 2), (rows, 1), 0, top)
    return jnp.take_along_axis(grid, (jnp.arange(top)[None, :] + offset_by) % top, axis=1)


def load_shares(amount, total, bound, lean, full):
    loads = [(1 << 20) // math.isqrt(grade ** lean) + 1 for grade in range(1, amount + 1)]
    largest = bound if full else min(bound, max(-(-total // amount), total * loads[0] // sum(loads)))
    least = 1 if total - largest >= amount - 1 else 0
    holding, rest = [largest] + [least] * (amount - 1), total - largest - least * (amount - 1)
    while rest > 0:
        free = [i for i in range(1, amount) if holding[i] < largest] or [i for i in range(1, amount) if holding[i] < bound]
        pool, budget = sum([loads[i] for i in free]), rest
        for i in free:
            addition = min(bound - holding[i], max(1, budget * loads[i] // pool), rest)
            holding[i] = holding[i] + addition
            rest = rest - addition
    return np.array(holding)


def gaussian(key, shape, deviation, limit, split=(), held_as=jnp.bfloat16):
    drawn = deviation * jax.random.normal(key, shape, jnp.float32)
    if split:
        drawn = drawn * steps_of(key, shape, split, -0.22, 0.18)
    return jnp.clip(drawn, -limit, limit).astype(held_as)


def setup_inputs(seed: int = 0) -> dict:
    key_list = jax.random.split(jax.random.key(seed), 12)
    acts = gaussian(key_list[0], (SLIDES, LEN, D), 1.0, 6.0, ((0, 2), (1, 16)))
    queries = draw_queries(jax.random.fold_in(key_list[11], 71), 0)
    keys = draw_keys(jax.random.fold_in(key_list[11], 71), 0)
    values = gaussian(key_list[3], (SLIDES, LEN, D), 1.0, 6.0, ((0, 2), (1, 16)))
    grad_out = gaussian(key_list[4], (SLIDES, LEN, D), 1.0, 6.0, ((0, 2), (1, 16)))
    gain = jnp.clip(1.0 + 0.1 * jax.random.normal(key_list[5], (D,), jnp.float32), 0.5, 1.5)
    router = gaussian(key_list[6], (D, EXPERTS), D ** -0.5, 0.1875)
    w_in = gaussian(key_list[7], (EXPERTS, FF, D), D ** -0.5, 0.1875, ((0, 2), (1, 16)))
    w_out = gaussian(key_list[8], (EXPERTS, FF, D), FF ** -0.5, 0.125, ((0, 2), (1, 16)))
    routes_keys = jax.random.split(jax.random.fold_in(key_list[9], 1), SLIDES * LEN // TOK_DEV)
    routes_turns = jax.random.permutation(jax.random.fold_in(key_list[9], 3), SLIDES * LEN // TOK_DEV)
    routes = jax.vmap(lambda own, number: routed_block(jax.random.fold_in(key_list[9], 2), own, number, TOK_DEV, EXPERTS, 1, CAP, 2))(routes_keys, routes_turns).reshape((SLIDES, LEN, 1))
    tissue = with_ends((jax.random.randint(key_list[10], (SLIDES, NBLOCKS), 0, 4) < 3).astype(jnp.int32), jax.random.fold_in(key_list[10], 1), 0, 1)
    return dict(acts=acts, queries=queries, keys=keys, values=values, grad_out=grad_out, gain=gain, router=router, w_in=w_in, w_out=w_out, routes=routes, tissue=tissue)


EPS = 1e-06

def gelu_tanh(value):
    return jax.nn.gelu(value, approximate=True)

def window_allow(place, tissue_row, tok, length):
    queries_at = place * tok + jnp.arange(tok)
    keys_at = place * tok - REACH + jnp.arange(tok + 2 * REACH)
    inside = (keys_at >= 0) & (keys_at < length)
    block_of = jnp.clip(keys_at, 0, length - 1) // BLOCK
    live = tissue_row[block_of] == 1
    near = jnp.abs(queries_at[:, None] - keys_at[None, :]) <= REACH
    same = queries_at[:, None] == keys_at[None, :]
    return near & inside[None, :] & (live[None, :] | same)

def head_probs(q_rows, k_rows, allow):
    heads = q_rows.shape[1] // HEAD
    q_heads = q_rows.astype(jnp.float32).reshape(q_rows.shape[0], heads, HEAD)
    k_heads = k_rows.astype(jnp.float32).reshape(k_rows.shape[0], heads, HEAD)
    scores = jnp.einsum('qhd,khd->hqk', q_heads, k_heads) * HEAD ** (-0.5)
    scores = jnp.where(allow[None], scores, -jnp.inf)
    top = lax.optimization_barrier(jnp.max(scores, -1, keepdims=True))
    weights = jnp.exp(scores - top)
    return weights / lax.optimization_barrier(jnp.sum(weights, -1, keepdims=True))

def front(x_rows, q_rows, ext, route_rows, tissue_row, place, gain, router):
    allow = window_allow(place, tissue_row, TOK_DEV, LEN)
    probs = head_probs(q_rows, ext[:, :D], allow)
    v_heads = ext[:, D:].astype(jnp.float32).reshape(-1, HEADS, HEAD)
    attn = jnp.einsum('hqk,khd->qhd', probs.astype(jnp.bfloat16).astype(jnp.float32), v_heads).reshape(TOK_DEV, D)
    mid = x_rows.astype(jnp.float32) + attn
    rms = lax.rsqrt(lax.optimization_barrier(jnp.mean(mid * mid, -1, keepdims=True)) + EPS)
    normed = mid * rms
    inner = (normed * gain[None, :]).astype(jnp.bfloat16)
    logits = jnp.dot(inner, router, preferred_element_type=jnp.float32)
    chance = jax.nn.softmax(logits, -1)
    onehot = (route_rows[:, None] == jnp.arange(EXPERTS)[None, :]).astype(jnp.int32)
    pick = lax.optimization_barrier(jnp.sum(chance * onehot.astype(jnp.float32), -1))
    before = jnp.cumsum(onehot, 0) - onehot
    rank = lax.optimization_barrier(jnp.sum(before * onehot, -1))
    table = onehot[:, :, None] * (rank[:, None, None] == jnp.arange(CAP)[None, None, :]).astype(jnp.int32)
    disp = table.reshape(TOK_DEV, EXPERTS * CAP).astype(jnp.bfloat16)
    return (allow, probs, normed, rms, inner, chance, onehot, pick, disp)

def reference(acts, queries, keys, values, grad_out, gain, router, w_in, w_out, routes, tissue):
    devices = SLIDES * N_SEQ
    joined = jnp.concatenate([keys, values], 2)
    padded = jnp.pad(joined, ((0, 0), (REACH, REACH), (0, 0)))
    x_dev = acts.reshape(devices, TOK_DEV, D)
    q_dev = queries.reshape(devices, TOK_DEV, D)
    g_dev = grad_out.reshape(devices, TOK_DEV, D)
    r_dev = routes.reshape(devices, TOK_DEV)

    def ext_of(dev):
        slide = dev // N_SEQ
        place = dev % N_SEQ
        return (lax.dynamic_slice(padded, (slide, place * TOK_DEV, 0), (1, TOK_DEV + 2 * REACH, 2 * D))[0], slide, place)

    def phase_send(items):
        dev, x_rows, q_rows, g_rows, route_rows = items
        ext, slide, place = ext_of(dev)
        tissue_row = lax.dynamic_index_in_dim(tissue, slide, 0, keepdims=False)
        outs = front(x_rows, q_rows, ext, route_rows, tissue_row, place, gain, router)
        disp = outs[8].astype(jnp.float32)
        send_u = jnp.einsum('tr,td->rd', disp, outs[4].astype(jnp.float32)).astype(jnp.bfloat16)
        send_g = jnp.einsum('tr,td->rd', disp, g_rows.astype(jnp.float32)).astype(jnp.bfloat16)
        return (send_u.reshape(EXPERTS, CAP, D), send_g.reshape(EXPERTS, CAP, D))
    slots_u, slots_g = lax.map(phase_send, (jnp.arange(devices), x_dev, q_dev, g_dev, r_dev))

    def expert_work(items):
        rows_u, rows_g, weight_in, weight_out = items
        flat_u = rows_u.reshape(devices * CAP, D)
        flat_g = rows_g.reshape(devices * CAP, D)
        hidden = jnp.dot(flat_u, weight_in.T, preferred_element_type=jnp.float32)
        act = gelu_tanh(hidden).astype(jnp.bfloat16)
        expert_out = jnp.dot(act, weight_out, preferred_element_type=jnp.float32)
        back_act = jnp.dot(flat_g, weight_out.T, preferred_element_type=jnp.float32)
        back_hidden = jax.vjp(gelu_tanh, hidden)[1](back_act)[0].astype(jnp.bfloat16)
        back_inner = jnp.dot(back_hidden, weight_in, preferred_element_type=jnp.float32).astype(jnp.bfloat16)
        grad_pick = lax.optimization_barrier(jnp.sum(flat_g.astype(jnp.float32) * expert_out, -1))
        return (back_inner.reshape(devices, CAP, D), grad_pick.reshape(devices, CAP))
    back_u, back_p = lax.map(expert_work, (jnp.moveaxis(slots_u, 1, 0), jnp.moveaxis(slots_g, 1, 0), w_in, w_out))
    back_u = jnp.moveaxis(back_u, 0, 1)
    back_p = jnp.moveaxis(back_p, 0, 1)

    def phase_back(items):
        dev, x_rows, q_rows, g_rows, route_rows, rows_back, picks_back = items
        ext, slide, place = ext_of(dev)
        tissue_row = lax.dynamic_index_in_dim(tissue, slide, 0, keepdims=False)
        allow, probs, normed, rms, inner, chance, onehot, pick, disp = front(x_rows, q_rows, ext, route_rows, tissue_row, place, gain, router)
        part_inner = jnp.dot(disp, rows_back.reshape(EXPERTS * CAP, D), preferred_element_type=jnp.float32)
        grad_pick = jnp.dot(disp.astype(jnp.float32), picks_back.reshape(EXPERTS * CAP), precision=lax.Precision.HIGHEST)
        grad_logits = (grad_pick * pick)[:, None] * (onehot.astype(jnp.float32) - chance)
        grad_inner = pick[:, None] * part_inner + jnp.dot(grad_logits, router.astype(jnp.float32).T, precision=lax.Precision.HIGHEST)
        router_term = jnp.dot(inner.astype(jnp.float32).T, grad_logits, precision=lax.Precision.HIGHEST)
        gain_term = lax.optimization_barrier(jnp.sum(grad_inner * normed, 0))
        grad_normed = grad_inner * gain[None, :]
        grad_mid = rms * (grad_normed - normed * lax.optimization_barrier(jnp.mean(grad_normed * normed, -1, keepdims=True))) + g_rows.astype(jnp.float32)
        grad_x = grad_mid.astype(jnp.bfloat16)
        q_heads = q_rows.astype(jnp.float32).reshape(TOK_DEV, HEADS, HEAD)
        k_heads = ext[:, :D].astype(jnp.float32).reshape(-1, HEADS, HEAD)
        v_heads = ext[:, D:].astype(jnp.float32).reshape(-1, HEADS, HEAD)
        o_heads = grad_x.astype(jnp.float32).reshape(TOK_DEV, HEADS, HEAD)
        probs_b = probs.astype(jnp.bfloat16).astype(jnp.float32)
        grad_v = jnp.einsum('hqk,qhd->khd', probs_b, o_heads).reshape(-1, D)
        grad_probs = jnp.einsum('qhd,khd->hqk', o_heads, v_heads)
        delta = lax.optimization_barrier(jnp.sum(probs * grad_probs, -1, keepdims=True))
        grad_scores = (probs * (grad_probs - delta) * HEAD ** (-0.5)).astype(jnp.bfloat16).astype(jnp.float32)
        grad_q = jnp.einsum('hqk,khd->qhd', grad_scores, k_heads).reshape(TOK_DEV, D).astype(jnp.bfloat16)
        grad_k = jnp.einsum('hqk,qhd->khd', grad_scores, q_heads).reshape(-1, D)
        both = jnp.concatenate([grad_k, grad_v], 1)
        own = both[REACH:REACH + TOK_DEV]
        low_rim = both[:REACH].astype(jnp.bfloat16)
        high_rim = both[REACH + TOK_DEV:].astype(jnp.bfloat16)
        return (grad_x, grad_q, own, low_rim, high_rim, router_term, gain_term)
    grad_x, grad_q, own, low_rim, high_rim, router_terms, gain_terms = lax.map(phase_back, (jnp.arange(devices), x_dev, q_dev, g_dev, r_dev, back_u, back_p))
    own = own.reshape(SLIDES, N_SEQ, TOK_DEV, 2 * D)
    low_rim = low_rim.reshape(SLIDES, N_SEQ, REACH, 2 * D).astype(jnp.float32)
    high_rim = high_rim.reshape(SLIDES, N_SEQ, REACH, 2 * D).astype(jnp.float32)
    empty = jnp.zeros((SLIDES, 1, REACH, 2 * D), jnp.float32)
    from_next = jnp.concatenate([low_rim[:, 1:], empty], 1)
    from_prev = jnp.concatenate([empty, high_rim[:, :-1]], 1)
    total = own + jnp.pad(from_prev, ((0, 0), (0, 0), (0, TOK_DEV - REACH), (0, 0)))
    total = total + jnp.pad(from_next, ((0, 0), (0, 0), (TOK_DEV - REACH, 0), (0, 0)))
    total = total.reshape(SLIDES, LEN, 2 * D)
    grad_keys = total[:, :, :D].astype(jnp.bfloat16)
    grad_values = total[:, :, D:].astype(jnp.bfloat16)
    return (grad_x.reshape(SLIDES, LEN, D), grad_q.reshape(SLIDES, LEN, D), grad_keys, grad_values, lax.optimization_barrier(jnp.sum(router_terms, 0)), lax.optimization_barrier(jnp.sum(gain_terms, 0)))
```

```python
import functools

import jax
import jax.numpy as jnp
from jax import lax
from jax.experimental import pallas as pl
from jax.experimental.pallas import tpu as pltpu
from jax.sharding import PartitionSpec as P

HEAD = 64
REACH = 128
BLOCK = 512
EPS = 1e-06
LANES = 128
NEG = -1e30
GELU_C = 0.7978845608028654
GELU_A = 0.044715
MESH = pl.DeviceIdType.MESH


def dot(a, b, contract, precision=None):
    return lax.dot_general(
        a, b, (contract, ((), ())), preferred_element_type=jnp.float32, precision=precision
    )


def flip(index, mask):
    size = 1
    while size <= mask:
        if mask & size:
            index = index + size - 2 * size * ((index // size) % 2)
        size *= 2
    return index


def reduce_rounds(n, experts):
    bits = [(1 << b, 0) for b in range((experts - 1).bit_length())]
    bits += [(0, 1 << b) for b in range((n - 1).bit_length())]
    rounds = []
    for start in range(0, len(bits), 3):
        masks = [(0, 0)]
        for e, m in bits[start : start + 3]:
            masks += [(a + e, b + m) for a, b in masks]
        rounds.append(masks[1:])
    return rounds


def kernel(
    n, experts, cap, nblocks, groups,
    acts_h, queries_h, keys, values, grad_out_h, gain, router, w_in, w_out, routes, tissue,
    grad_acts_h, grad_q_h, grad_k_h, grad_v_h, small_out,
    acts, queries, grad_out, grad_acts, grad_q, grad_k, grad_v, act_s, slope_s,
    weights, kx, vx, bias, probs, attn, normed_s, u_send, u_slots, g_send, g_slots,
    inner_acc, pick_acc, b_send, b_slots, p_send, p_slots, own_kv,
    low_send, high_send, low_recv, high_recv, red_send, red_recv,
    local_sem, out_sem, halo_ss, halo_rs, w_ss, w_rs, ex_ss, ex_rs, rim_ss, rim_rs, red_ss, red_rs,
):
    tok, width = acts_h.shape
    span = tok + 2 * REACH
    frows = w_in.shape[0]
    rows = experts * cap
    pairs = width // LANES
    place = lax.axis_index("seq")
    me = lax.axis_index("expert")
    structured = n == 16
    bf16, f32 = jnp.bfloat16, jnp.float32

    def at(expert, seq):
        return (expert, seq)

    def remote(src, dst, ss, rs, where):
        return pltpu.make_async_remote_copy(
            src_ref=src, dst_ref=dst, send_sem=ss, recv_sem=rs, device_id=where, device_id_type=MESH
        )

    barrier = pltpu.get_barrier_semaphore()
    rounds = reduce_rounds(n, experts)
    peers = [at(flip(me, e), flip(place, m)) for masks in rounds for e, m in masks]
    if structured:
        z = place // 4
        peers += [at(me, (place + 1) % n), at(me, (place + n - 1) % n)]
    else:
        peers += [at(me, (place + d) % n) for d in range(1, n)]
        peers += [at((me + d) % experts, place) for d in range(1, experts)]
    for peer in peers:
        pl.semaphore_signal(barrier, inc=1, device_id=peer, device_id_type=MESH)

    own_copies = [
        pltpu.make_async_copy(w_in, weights.at[place, 0], local_sem.at[0]),
        pltpu.make_async_copy(w_out, weights.at[place, 1], local_sem.at[1]),
        pltpu.make_async_copy(keys, kx.at[pl.ds(REACH, tok)], local_sem.at[2]),
        pltpu.make_async_copy(values, vx.at[pl.ds(REACH, tok)], local_sem.at[3]),
        pltpu.make_async_copy(grad_out_h, grad_out, local_sem.at[4]),
        pltpu.make_async_copy(queries_h, queries, local_sem.at[5]),
        pltpu.make_async_copy(acts_h, acts, local_sem.at[6]),
    ]
    for copy in own_copies:
        copy.start()
    lane = lax.broadcasted_iota(jnp.int32, (tok, LANES), 1)
    row_at = lax.broadcasted_iota(jnp.int32, (tok, tok), 0)
    col_at = lax.broadcasted_iota(jnp.int32, (tok, tok), 1)
    spread_routes = jnp.where(row_at == col_at, jnp.broadcast_to(routes[...], (tok, tok)), 0)
    route = jnp.sum(spread_routes.astype(f32), -1, keepdims=True).astype(jnp.int32)
    onehot = (route == lane).astype(f32)
    lower = (row_at > col_at).astype(bf16)
    before = dot(lower, onehot.astype(bf16), ((1,), (0,)))
    rank = jnp.sum(before * onehot, -1, keepdims=True).astype(jnp.int32)
    slot = route * cap + rank
    disp = (slot == lax.broadcasted_iota(jnp.int32, (tok, rows), 1)).astype(bf16)

    here = (place // 2) % 2 if structured else 0
    q_at = place * tok + lax.broadcasted_iota(jnp.int32, (tok, span), 0)
    k_at = place * tok - REACH + lax.broadcasted_iota(jnp.int32, (tok, span), 1)
    live = jnp.zeros((tok, span), jnp.int32)
    for b in range(nblocks):
        live = jnp.where((k_at >= b * BLOCK) & (k_at < (b + 1) * BLOCK), tissue[0, b], live)
    near_by = jnp.abs(q_at - k_at) <= REACH
    allow = near_by & (k_at >= 0) & (k_at < n * tok) & ((live == 1) | (q_at == k_at))
    bias[...] = jnp.where(allow, 0.0, NEG).astype(f32)
    own_copies[4].wait()
    moved_g = dot(disp, grad_out[...], ((0,), (0,))).astype(bf16)
    g_send[...] = moved_g.reshape(experts, cap, width)
    g_slots[here, me] = g_send[me]
    pl.semaphore_wait(barrier, len(peers))

    up, down = at(me, (place + 1) % n), at(me, (place + n - 1) % n)
    to_up = [
        remote(src, dst.at[pl.ds(0, REACH)], halo_ss.at[i, 0], halo_rs.at[i, 0], up)
        for i, (src, dst) in enumerate(((keys, kx), (values, vx)))
    ]
    to_down = [
        remote(src, dst.at[pl.ds(REACH + tok, REACH)], halo_ss.at[i, 1], halo_rs.at[i, 1], down)
        for i, (src, dst) in enumerate(((keys, kx), (values, vx)))
    ]

    @pl.when(place < n - 1)
    def _():
        for copy in to_up:
            copy.start()

    @pl.when(place > 0)
    def _():
        for copy in to_down:
            copy.start()

    def push(owner, j, kind, step, where, src=None):
        return remote(
            weights.at[owner, j] if src is None else src,
            weights.at[owner, j],
            w_ss.at[kind, step, j],
            w_rs.at[owner, j],
            where,
        )

    def landed(owner, j):
        push(owner, j, 0, 0, up).wait_recv()

    mine = (w_in, w_out)
    if structured:
        x = (place // 2) % 2
        low = place % 4
        middle = (z == 1) | (z == 2)
        near, far = flip(place, 4), flip(place, 12)
        other_c = flip(place, 1)

        def column(k):
            return jnp.where(
                k == 0, z, jnp.where(k == 1, z + 1 - 2 * (z % 2), jnp.where(k == 2, 2 - z // 2, 3 - 3 * (z // 2)))
            )

        for j in range(2):
            push(place, j, 0, 0, at(me, near), mine[j]).start()

        @pl.when(middle)
        def _():
            for j in range(2):
                push(place, j, 1, 0, at(me, far), mine[j]).start()

        for j in range(2):
            push(place, j, 2, 0, at(me, other_c), mine[j]).start()
    else:

        def spread(d, carry):
            for j in range(2):
                push(place, j, 0, d, at(me, (place + d) % n), mine[j]).start()
            return carry

        lax.fori_loop(1, n, spread, 0)

    offsets = [(dx, d) for dx in range(groups) for d in range(experts)][1:]

    def beside(dx, d):
        return at((me + d) % experts, flip(place, 2 * dx))

    def exchange(piece, slots, which):
        return [
            remote(
                piece(here + dx * (1 - 2 * here), (me + d) % experts),
                slots.at[here, me],
                ex_ss.at[which, dx * experts + d],
                ex_rs.at[which, here * experts + me],
                beside(dx, d),
            )
            for dx, d in offsets
        ]

    def arrivals(slots, which):
        for dx, d in offsets:
            group, source = here + dx * (1 - 2 * here), (me + d) % experts
            remote(
                slots.at[group, source],
                slots.at[group, source],
                ex_ss.at[which, dx * experts + d],
                ex_rs.at[which, group * experts + source],
                beside(dx, d),
            ).wait_recv()

    half = lax.broadcasted_iota(jnp.int32, (tok, LANES), 1) < HEAD
    first = half.astype(bf16)
    second = (1.0 - half.astype(f32)).astype(bf16)

    def stack(value):
        return jnp.concatenate([value * first, value * second], 0)

    own_copies[2].wait()
    own_copies[3].wait()

    @pl.when(place > 0)
    def _():
        for copy in to_up:
            copy.wait_recv()

    @pl.when(place == 0)
    def _():
        kx[pl.ds(0, REACH), :] = jnp.zeros((REACH, width), bf16)
        vx[pl.ds(0, REACH), :] = jnp.zeros((REACH, width), bf16)

    @pl.when(place < n - 1)
    def _():
        for copy in to_down:
            copy.wait_recv()

    @pl.when(place == n - 1)
    def _():
        kx[pl.ds(REACH + tok, REACH), :] = jnp.zeros((REACH, width), bf16)
        vx[pl.ds(REACH + tok, REACH), :] = jnp.zeros((REACH, width), bf16)

    sends_g = exchange(lambda group, expert: g_send.at[expert], g_slots, 0)
    for copy in sends_g:
        copy.start()
    own_copies[5].wait()

    if structured:

        def relay(k):
            owner = column(k) * 4 + low
            for j in range(2):
                landed(owner, j)

                @pl.when(middle)
                def _():
                    push(owner, j, 0, k, at(me, jnp.where(k == 1, far, near))).start()

                push(owner, j, 2, k, at(me, other_c)).start()

        relay(1)

        @pl.when(middle)
        def _():
            relay(2)

    def forward(i, carry):
        cols = pl.ds(pl.multiple_of(i * LANES, LANES), LANES)
        scores = dot(stack(queries[:, cols]), kx[:, cols], ((1,), (1,))) * HEAD ** (-0.5)
        both = jnp.concatenate([bias[...], bias[...]], 0)
        scores = scores + both
        weight = jnp.exp(scores - jnp.max(scores, -1, keepdims=True))
        prob = weight / jnp.sum(weight, -1, keepdims=True)
        probs[i] = prob
        mixed = dot(prob.astype(bf16), vx[:, cols], ((1,), (0,)))
        attn[:, cols] = jnp.where(half, mixed[:tok], mixed[tok:])
        return carry

    lax.fori_loop(0, pairs, forward, 0)

    own_copies[6].wait()
    mid = acts[...].astype(f32) + attn[...]
    rms = lax.rsqrt(jnp.mean(mid * mid, -1, keepdims=True) + EPS)
    normed_s[...] = mid * rms
    inner = (normed_s[...] * gain[...]).astype(bf16)
    moved_u = dot(disp, inner, ((0,), (0,))).astype(bf16)
    u_send[...] = moved_u.reshape(experts, cap, width)
    u_slots[here, me] = u_send[me]
    sends_u = exchange(lambda group, expert: u_send.at[expert], u_slots, 1)
    for copy in sends_u:
        copy.start()

    inner_f = inner.astype(f32)
    router_f = router[...].astype(f32)
    r_lane = lane
    logits = jnp.full((tok, LANES), NEG, f32)
    for e in range(experts):
        logits = jnp.where(lane == e, jnp.sum(inner_f * router_f[e : e + 1, :], -1, keepdims=True), logits)
    chance = jnp.exp(logits - jnp.max(logits, -1, keepdims=True))
    chance = chance / jnp.sum(chance, -1, keepdims=True)
    chosen = (route == r_lane).astype(f32)
    pick = jnp.sum(chance * chosen, -1, keepdims=True)

    own_copies[0].wait()
    own_copies[1].wait()
    inner_acc[...] = jnp.zeros_like(inner_acc)
    pick_acc[...] = jnp.zeros_like(pick_acc)
    per = max(1, 256 // frows)

    span_w = per * frows

    def first_half(start):
        wi = weights[pl.ds(start, per), 0].reshape(span_w, width)
        hidden = dot(u_slots[...].reshape(groups * rows, width), wi, ((1,), (1,)))
        square = hidden * hidden
        t = jnp.tanh(GELU_C * hidden * (1.0 + GELU_A * square))
        gate = 0.5 * (1.0 + t)
        act = (hidden * gate).astype(bf16).astype(f32)
        slope = gate + 0.5 * hidden * (1.0 - t * t) * (GELU_C * (1.0 + 3.0 * GELU_A * square))
        act_s[...] = act.reshape(groups, rows, span_w)
        slope_s[...] = slope.reshape(groups, rows, span_w)

    def second_half(start):
        wi = weights[pl.ds(start, per), 0].reshape(span_w, width)
        wo = weights[pl.ds(start, per), 1].reshape(span_w, width)
        back = dot(g_slots[...].reshape(groups * rows, width), wo, ((1,), (1,)))
        act = act_s[...].reshape(groups * rows, span_w)
        slope = slope_s[...].reshape(groups * rows, span_w)
        pick_acc[...] += jnp.sum(act * back, -1, keepdims=True).reshape(groups, rows, 1)
        inner_acc[...] += dot((back * slope).astype(bf16), wi, ((1,), (0,))).reshape(groups, rows, width)

    eye = (
        lax.broadcasted_iota(jnp.int32, (cap, LANES), 0) == lax.broadcasted_iota(jnp.int32, (cap, LANES), 1)
    ).astype(f32)

    def last_half(start, group):
        wi = weights[pl.ds(start, per), 0].reshape(span_w, width)
        wo = weights[pl.ds(start, per), 1].reshape(span_w, width)
        back = dot(g_slots[group].reshape(rows, width), wo, ((1,), (1,)))
        picked = pick_acc[group] + jnp.sum(act_s[group] * back, -1, keepdims=True)
        total = inner_acc[group] + dot((back * slope_s[group]).astype(bf16), wi, ((1,), (0,)))
        b_send[group] = total.astype(bf16).reshape(experts, cap, width)
        for e in range(experts):
            line = jnp.sum(picked[e * cap : (e + 1) * cap] * eye, 0, keepdims=True)
            p_send[group, e] = jnp.broadcast_to(line, (8, LANES))

    sends_b = exchange(lambda group, expert: b_send.at[group, expert], b_slots, 2)
    sends_p = exchange(lambda group, expert: p_send.at[group, expert], p_slots, 3)

    def give_back(wanted):
        for (dx, d), p_copy, b_copy in list(zip(offsets, sends_p, sends_b))[::-1]:
            if dx in wanted:
                p_copy.start()
                b_copy.start()

    if structured:

        @pl.when(middle)
        def _():
            relay(3)

        @pl.when(jnp.logical_not(middle))
        def _():
            relay(2)

        arrivals(g_slots, 0)
        arrivals(u_slots, 1)

        def step(k, carry):
            start = column(k) * 4 + x * 2
            landed(start + 1 - place % 2, 0)
            first_half(start)
            landed(start + 1 - place % 2, 1)
            second_half(start)
            return carry

        lax.fori_loop(0, 3, step, 0)

        @pl.when(jnp.logical_not(middle))
        def _():
            relay(3)

        start = column(3) * 4 + x * 2
        landed(start + 1 - place % 2, 0)
        first_half(start)
        landed(start + 1 - place % 2, 1)
    else:

        def settle(d, carry):
            for j in range(2):
                landed((place + d) % n, j)
            return carry

        lax.fori_loop(1, n, settle, 0)
        arrivals(g_slots, 0)
        arrivals(u_slots, 1)

        def step(j, carry):
            first_half(j * per)
            second_half(j * per)
            return carry

        lax.fori_loop(0, n // per - 1, step, 0)
        start = n - per
        first_half(start)

    for dx in range(groups)[::-1]:
        last_half(start, here + dx * (1 - 2 * here))
        give_back((dx,))

    b_slots[here, me] = b_send[here, me]
    p_slots[here, me] = p_send[here, me]
    arrivals(p_slots, 3)
    arrivals(b_slots, 2)

    normed = normed_s[...]
    part_inner = dot(disp, b_slots[0].reshape(rows, width), ((1,), (0,)))
    for group in range(1, groups):
        part_inner = part_inner + dot(disp, b_slots[group].reshape(rows, width), ((1,), (0,)))
    picks = jnp.zeros((tok, LANES), f32)
    for e in range(experts):
        line = p_slots[0, e, :1, :]
        for group in range(1, groups):
            line = line + p_slots[group, e, :1, :]
        picks = jnp.where(route == e, line, picks)
    grad_pick = jnp.sum(jnp.where(rank == lane, picks, 0.0), -1, keepdims=True)
    grad_logits = (grad_pick * pick) * (chosen - chance)
    grad_inner = pick * part_inner

    def pack(at_row, line):
        for c in range(pairs):
            where = at_row * pairs + c
            red_send[0, where : where + 1, :] = line[:, c * LANES : (c + 1) * LANES]

    inner_f = (normed * gain[...]).astype(bf16).astype(f32)
    for e in range(experts):
        column_e = grad_logits[:, e : e + 1]
        grad_inner = grad_inner + column_e * router_f[e : e + 1, :]
        pack(e, jnp.sum(inner_f * column_e, 0, keepdims=True))
    pack(experts, jnp.sum(grad_inner * normed, 0, keepdims=True))
    grad_normed = grad_inner * gain[...]
    grad_mid = rms * (
        grad_normed - normed * jnp.mean(grad_normed * normed, -1, keepdims=True)
    ) + grad_out[...].astype(f32)
    grad_acts[...] = grad_mid.astype(bf16)
    results = [
        pltpu.make_async_copy(source, target, out_sem.at[i])
        for i, (source, target) in enumerate(
            ((grad_acts, grad_acts_h), (grad_q, grad_q_h), (grad_k, grad_k_h), (grad_v, grad_v_h))
        )
    ]
    results[0].start()

    reduces = [
        [
            remote(red_send.at[j], red_recv.at[j, i], red_ss.at[j, i], red_rs.at[j, i], at(flip(me, e), flip(place, m)))
            for i, (e, m) in enumerate(masks)
        ]
        for j, masks in enumerate(rounds)
    ]

    def reduce_step(j):
        total = red_send[j]
        for i, copy in enumerate(reduces[j]):
            copy.wait_recv()
            total = total + red_recv[j, i]
        if j + 1 < len(reduces):
            red_send[j + 1] = total
            for copy in reduces[j + 1]:
                copy.start()
        else:
            small_out[...] = total

    for copy in reduces[0]:
        copy.start()

    def rim_down(i):
        return remote(low_send.at[i], low_recv.at[i], rim_ss.at[0, i], rim_rs.at[0, i], down)

    def rim_up(i):
        return remote(high_send.at[i], high_recv.at[i], rim_ss.at[1, i], rim_rs.at[1, i], up)

    def backward(i, carry):
        for j in range(len(reduces) - 1):

            @pl.when(i == 4 + j)
            def _():
                reduce_step(j)

        cols = pl.ds(pl.multiple_of(i * LANES, LANES), LANES)
        o_stack = stack(grad_acts[:, cols])
        q_stack = stack(queries[:, cols])
        prob = probs[i]
        grad_probs = dot(o_stack, vx[:, cols], ((1,), (1,)))
        value_terms = dot(prob.astype(bf16), o_stack, ((0,), (0,)))
        delta = jnp.sum(prob * grad_probs, -1, keepdims=True)
        grad_scores = (prob * (grad_probs - delta) * HEAD ** (-0.5)).astype(bf16)
        query_terms = dot(grad_scores, kx[:, cols], ((1,), (0,)))
        grad_q[:, cols] = jnp.where(half, query_terms[:tok], query_terms[tok:]).astype(bf16)
        key_terms = dot(grad_scores, q_stack, ((0,), (0,)))
        for slot_at, terms in enumerate((key_terms, value_terms)):
            low_send[i, slot_at] = terms[:REACH].astype(bf16)
            own_kv[slot_at, :, cols] = terms[REACH : REACH + tok]
            high_send[i, slot_at] = terms[REACH + tok :].astype(bf16)

        @pl.when(place > 0)
        def _():
            rim_down(i).start()

        @pl.when(place < n - 1)
        def _():
            rim_up(i).start()

        return carry

    lax.fori_loop(0, pairs, backward, 0)
    results[1].start()

    def finish(i, carry):
        cols = pl.ds(pl.multiple_of(i * LANES, LANES), LANES)

        @pl.when(place > 0)
        def _():
            rim_up(i).wait_recv()
            for slot_at in range(2):
                own_kv[slot_at, :REACH, cols] += high_recv[i, slot_at].astype(f32)

        @pl.when(place < n - 1)
        def _():
            rim_down(i).wait_recv()
            for slot_at in range(2):
                own_kv[slot_at, tok - REACH :, cols] += low_recv[i, slot_at].astype(f32)

        grad_k[:, cols] = own_kv[0, :, cols].astype(bf16)
        grad_v[:, cols] = own_kv[1, :, cols].astype(bf16)
        return carry

    lax.fori_loop(0, pairs, finish, 0)
    results[2].start()
    results[3].start()
    reduce_step(len(reduces) - 1)

    @pl.when(place < n - 1)
    def _():
        for copy in to_up:
            copy.wait_send()

    @pl.when(place > 0)
    def _():
        for copy in to_down:
            copy.wait_send()

    for copy in sends_g + sends_u + sends_b + sends_p + [c for group in reduces for c in group]:
        copy.wait_send()

    def drain(i, carry):
        @pl.when(place > 0)
        def _():
            rim_down(i).wait_send()

        @pl.when(place < n - 1)
        def _():
            rim_up(i).wait_send()

        return carry

    lax.fori_loop(0, pairs, drain, 0)
    if structured:
        for j in range(2):
            push(place, j, 0, 0, at(me, near), mine[j]).wait_send()

        @pl.when(middle)
        def _():
            for j in range(2):
                push(place, j, 1, 0, at(me, far), mine[j]).wait_send()

        def sent(k, carry):
            for j in range(2):

                @pl.when((k > 0) & middle)
                def _():
                    push(place, j, 0, k, at(me, near)).wait_send()

                push(place, j, 2, k, at(me, near)).wait_send()
            return carry

        lax.fori_loop(0, 4, sent, 0)
    else:

        def sent(d, carry):
            for j in range(2):
                push(place, j, 0, d, at(me, (place + d) % n), mine[j]).wait_send()
            return carry

        lax.fori_loop(1, n, sent, 0)
    for copy in results:
        copy.wait()


def shards(acts, queries, keys, values, grad_out, gain, router, w_in, w_out, routes, tissue):
    tok, width = acts.shape[1:]
    n = lax.axis_size("seq")
    experts = router.shape[1]
    cap = max(2, 5 * tok // (4 * experts))
    cap = -(-cap // 16) * 16
    rows = experts * cap
    frows = w_in.shape[1]
    span = tok + 2 * REACH
    pairs = width // LANES
    lines = (experts + 1) * pairs
    per = max(1, 256 // frows)
    rounds = reduce_rounds(n, experts)
    most = max(len(masks) for masks in rounds)
    groups = 2 if n == 16 else 1
    bf16, f32 = jnp.bfloat16, jnp.float32
    vmem = pl.BlockSpec(memory_space=pltpu.VMEM)
    hbm = pl.BlockSpec(memory_space=pl.ANY)
    big = jax.ShapeDtypeStruct((tok, width), bf16)
    dma = pltpu.SemaphoreType.DMA
    steps = 4 if n == 16 else n
    outs = pl.pallas_call(
        functools.partial(kernel, n, experts, cap, tissue.shape[1], groups),
        out_shape=[big, big, big, big, jax.ShapeDtypeStruct((lines, LANES), f32)],
        in_specs=[hbm] * 5 + [vmem] * 2 + [hbm] * 2 + [vmem, pl.BlockSpec(memory_space=pltpu.SMEM)],
        out_specs=[hbm] * 4 + [vmem],
        scratch_shapes=[pltpu.VMEM((tok, width), bf16)] * 7
        + [pltpu.VMEM((groups, rows, per * frows), f32)] * 2
        + [
            pltpu.VMEM((n, 2, frows, width), bf16),
            pltpu.VMEM((span, width), bf16),
            pltpu.VMEM((span, width), bf16),
            pltpu.VMEM((tok, span), f32),
            pltpu.VMEM((pairs, 2 * tok, span), f32),
            pltpu.VMEM((tok, width), f32),
            pltpu.VMEM((tok, width), f32),
            pltpu.VMEM((experts, cap, width), bf16),
            pltpu.VMEM((groups, experts, cap, width), bf16),
            pltpu.VMEM((experts, cap, width), bf16),
            pltpu.VMEM((groups, experts, cap, width), bf16),
            pltpu.VMEM((groups, rows, width), f32),
            pltpu.VMEM((groups, rows, 1), f32),
            pltpu.VMEM((groups, experts, cap, width), bf16),
            pltpu.VMEM((groups, experts, cap, width), bf16),
            pltpu.VMEM((groups, experts, 8, LANES), f32),
            pltpu.VMEM((groups, experts, 8, LANES), f32),
            pltpu.VMEM((2, tok, width), f32),
            pltpu.VMEM((pairs, 2, REACH, LANES), bf16),
            pltpu.VMEM((pairs, 2, REACH, LANES), bf16),
            pltpu.VMEM((pairs, 2, REACH, LANES), bf16),
            pltpu.VMEM((pairs, 2, REACH, LANES), bf16),
            pltpu.VMEM((len(rounds), lines, LANES), f32),
            pltpu.VMEM((len(rounds), most, lines, LANES), f32),
            dma((7,)),
            dma((4,)),
            dma((2, 2)),
            dma((2, 2)),
            dma((3, steps, 2)),
            dma((n, 2)),
            dma((4, groups * experts)),
            dma((4, groups * experts)),
            dma((2, pairs)),
            dma((2, pairs)),
            dma((len(rounds), most)),
            dma((len(rounds), most)),
        ],
        compiler_params=pltpu.CompilerParams(
            collective_id=0, has_side_effects=True, vmem_limit_bytes=60 * 1024 * 1024
        ),
    )(
        acts[0], queries[0], keys[0], values[0], grad_out[0], gain[None], router.T,
        w_in[0], w_out[0], routes[:, :, 0], tissue,
    )
    outs = pl.pallas_call(
        hand_out,
        out_shape=[
            big, big, big, big,
            jax.ShapeDtypeStruct((experts, width), f32), jax.ShapeDtypeStruct((1, width), f32),
        ],
        in_specs=[vmem] * 5,
        out_specs=[vmem] * 6,
    )(*outs)
    return tuple(out[None] for out in outs[:4]) + (outs[4].T, outs[5][0])


def hand_out(*refs):
    for source, target in zip(refs[:4], refs[5:9]):
        target[...] = source[...]
    small, experts = refs[4], refs[9].shape[0]
    pairs = small.shape[0] // (experts + 1)
    for row in range(experts + 1):
        target, line = (refs[9], row) if row < experts else (refs[10], 0)
        for c in range(pairs):
            where = row * pairs + c
            target[line : line + 1, c * LANES : (c + 1) * LANES] = small[where : where + 1, :]


def solution(mesh):
    tiles = P("expert", "seq", None)
    in_specs = (tiles,) * 5 + (P(), P()) + (tiles,) * 3 + (P("expert", None),)
    out_specs = (tiles,) * 4 + (P(), P())
    return jax.shard_map(shards, mesh=mesh, in_specs=in_specs, out_specs=out_specs, check_vma=False)
```

```python
import functools

import jax
import jax.numpy as jnp
from jax import lax
from jax.experimental import pallas as pl
from jax.experimental.pallas import tpu as pltpu
from jax.sharding import PartitionSpec as P

HEAD = 64
REACH = 128
BLOCK = 512
EPS = 1e-06
LANES = 128
NEG = -1e30
GELU_C = 0.7978845608028654
GELU_A = 0.044715
MESH = pl.DeviceIdType.MESH


def dot(a, b, contract, precision=None):
    return lax.dot_general(
        a, b, (contract, ((), ())), preferred_element_type=jnp.float32, precision=precision
    )


def flip(index, mask):
    size = 1
    while size <= mask:
        if mask & size:
            index = index + size - 2 * size * ((index // size) % 2)
        size *= 2
    return index


def reduce_rounds(n, experts):
    bits = [(1 << b, 0) for b in range((experts - 1).bit_length())]
    bits += [(0, 1 << b) for b in range((n - 1).bit_length())]
    rounds = []
    for start in range(0, len(bits), 3):
        masks = [(0, 0)]
        for e, m in bits[start : start + 3]:
            masks += [(a + e, b + m) for a, b in masks]
        rounds.append(masks[1:])
    return rounds


def kernel(
    n, experts, cap, nblocks, groups,
    acts_h, queries_h, keys, values, grad_out_h, gain, router, w_in, w_out, routes, tissue,
    grad_acts_h, grad_q_h, grad_k_h, grad_v_h, small_out,
    acts, queries, grad_out, grad_acts, grad_q, grad_k, grad_v, act_s, slope_s,
    weights, kx, vx, bias, probs, attn, normed_s, u_send, u_slots, g_send, g_slots,
    inner_acc, pick_acc, b_send, b_slots, p_send, p_slots, own_kv,
    stats, stat_send, stat_recv, side_bias, side_q, side_o, side_probs, red_send, red_recv,
    local_sem, out_sem, halo_ss, halo_rs, w_ss, w_rs, ex_ss, ex_rs, nb_ss, nb_rs, red_ss, red_rs,
):
    tok, width = acts_h.shape
    span = tok + 2 * REACH
    frows = w_in.shape[0]
    rows = experts * cap
    pairs = width // LANES
    place = lax.axis_index("seq")
    me = lax.axis_index("expert")
    structured = n == 16
    bf16, f32 = jnp.bfloat16, jnp.float32

    def at(expert, seq):
        return (expert, seq)

    def remote(src, dst, ss, rs, where):
        return pltpu.make_async_remote_copy(
            src_ref=src, dst_ref=dst, send_sem=ss, recv_sem=rs, device_id=where, device_id_type=MESH
        )

    barrier = pltpu.get_barrier_semaphore()
    rounds = reduce_rounds(n, experts)
    peers = [at(flip(me, e), flip(place, m)) for masks in rounds for e, m in masks]
    if structured:
        z = place // 4
        peers += [at(me, (place + 1) % n), at(me, (place + n - 1) % n)]
    else:
        peers += [at(me, (place + d) % n) for d in range(1, n)]
        peers += [at((me + d) % experts, place) for d in range(1, experts)]
    for peer in peers:
        pl.semaphore_signal(barrier, inc=1, device_id=peer, device_id_type=MESH)

    own_copies = [
        pltpu.make_async_copy(w_in, weights.at[place, 0], local_sem.at[0]),
        pltpu.make_async_copy(w_out, weights.at[place, 1], local_sem.at[1]),
        pltpu.make_async_copy(keys, kx.at[pl.ds(REACH, tok)], local_sem.at[2]),
        pltpu.make_async_copy(values, vx.at[pl.ds(REACH, tok)], local_sem.at[3]),
        pltpu.make_async_copy(grad_out_h, grad_out, local_sem.at[4]),
        pltpu.make_async_copy(queries_h, queries, local_sem.at[5]),
        pltpu.make_async_copy(acts_h, acts, local_sem.at[6]),
    ]
    for copy in own_copies:
        copy.start()
    lane = lax.broadcasted_iota(jnp.int32, (tok, LANES), 1)
    row_at = lax.broadcasted_iota(jnp.int32, (tok, tok), 0)
    col_at = lax.broadcasted_iota(jnp.int32, (tok, tok), 1)
    spread_routes = jnp.where(row_at == col_at, jnp.broadcast_to(routes[...], (tok, tok)), 0)
    route = jnp.sum(spread_routes.astype(f32), -1, keepdims=True).astype(jnp.int32)
    onehot = (route == lane).astype(f32)
    lower = (row_at > col_at).astype(bf16)
    before = dot(lower, onehot.astype(bf16), ((1,), (0,)))
    rank = jnp.sum(before * onehot, -1, keepdims=True).astype(jnp.int32)
    slot = route * cap + rank
    disp = (slot == lax.broadcasted_iota(jnp.int32, (tok, rows), 1)).astype(bf16)

    here = (place // 2) % 2 if structured else 0
    q_at = place * tok + lax.broadcasted_iota(jnp.int32, (tok, span), 0)
    k_at = place * tok - REACH + lax.broadcasted_iota(jnp.int32, (tok, span), 1)
    live = jnp.zeros((tok, span), jnp.int32)
    for b in range(nblocks):
        live = jnp.where((k_at >= b * BLOCK) & (k_at < (b + 1) * BLOCK), tissue[0, b], live)
    near_by = jnp.abs(q_at - k_at) <= REACH
    allow = near_by & (k_at >= 0) & (k_at < n * tok) & ((live == 1) | (q_at == k_at))
    bias[...] = jnp.where(allow, 0.0, NEG).astype(f32)
    live_own = live[:, REACH : REACH + tok] == 1
    for r, near_side in enumerate(((col_at <= row_at) & (place > 0), (row_at <= col_at) & (place < n - 1))):
        side_bias[r] = jnp.where(near_side & live_own, 0.0, NEG).astype(f32)
    own_copies[4].wait()
    moved_g = dot(disp, grad_out[...], ((0,), (0,))).astype(bf16)
    g_send[...] = moved_g.reshape(experts, cap, width)
    g_slots[here, me] = g_send[me]
    pl.semaphore_wait(barrier, len(peers))

    up, down = at(me, (place + 1) % n), at(me, (place + n - 1) % n)
    to_up = [
        remote(src, dst.at[pl.ds(0, REACH)], halo_ss.at[i, 0], halo_rs.at[i, 0], up)
        for i, (src, dst) in enumerate(((keys, kx), (values, vx)))
    ]
    to_down = [
        remote(src, dst.at[pl.ds(REACH + tok, REACH)], halo_ss.at[i, 1], halo_rs.at[i, 1], down)
        for i, (src, dst) in enumerate(((keys, kx), (values, vx)))
    ]

    heads = 2 * pairs
    targets = (up, down)
    has = (place < n - 1, place > 0)
    comes = (place > 0, place < n - 1)

    def half_rows(t):
        return pl.ds(t * pairs, pairs)

    def half_cols(t):
        return pl.ds(t * (width // 2), width // 2)

    def beside_copy(kind, way):
        if kind == 0:
            src, dst = queries_h, side_q.at[way]
        elif kind == 1:
            src, dst = stat_send.at[0], stat_recv.at[way, 0]
        elif kind < 4:
            src, dst = (stat_send.at[1, half_rows(kind - 2)], stat_recv.at[way, 1, half_rows(kind - 2)])
        else:
            src, dst = grad_acts.at[:, half_cols(kind - 4)], side_o.at[way, :, half_cols(kind - 4)]
        return remote(src, dst, nb_ss.at[kind, way], nb_rs.at[kind, way], targets[way])

    def tell(kinds, ways=(0, 1)):
        for way in ways:

            @pl.when(has[way])
            def _():
                for kind in kinds:
                    beside_copy(kind, way).start()

    def hear(kinds):
        for way in range(2):

            @pl.when(comes[way])
            def _():
                for kind in kinds:
                    beside_copy(kind, way).wait_recv()

    @pl.when(place < n - 1)
    def _():
        for copy in to_up:
            copy.start()

    @pl.when(place > 0)
    def _():
        for copy in to_down:
            copy.start()

    def push(owner, j, kind, step, where, src=None):
        return remote(
            weights.at[owner, j] if src is None else src,
            weights.at[owner, j],
            w_ss.at[kind, step, j],
            w_rs.at[owner, j],
            where,
        )

    def landed(owner, j):
        push(owner, j, 0, 0, up).wait_recv()

    mine = (w_in, w_out)
    if structured:
        x = (place // 2) % 2
        low = place % 4
        middle = (z == 1) | (z == 2)
        near, far = flip(place, 4), flip(place, 12)
        other_c = flip(place, 1)

        def column(k):
            return jnp.where(
                k == 0, z, jnp.where(k == 1, z + 1 - 2 * (z % 2), jnp.where(k == 2, 2 - z // 2, 3 - 3 * (z // 2)))
            )

        for j in range(2):
            push(place, j, 0, 0, at(me, near), mine[j]).start()

        @pl.when(middle)
        def _():
            for j in range(2):
                push(place, j, 1, 0, at(me, far), mine[j]).start()

        for j in range(2):
            push(place, j, 2, 0, at(me, other_c), mine[j]).start()
    else:

        def spread(d, carry):
            for j in range(2):
                push(place, j, 0, d, at(me, (place + d) % n), mine[j]).start()
            return carry

        lax.fori_loop(1, n, spread, 0)

    offsets = [(dx, d) for dx in range(groups) for d in range(experts)][1:]

    def beside(dx, d):
        return at((me + d) % experts, flip(place, 2 * dx))

    def exchange(piece, slots, which):
        return [
            remote(
                piece(here + dx * (1 - 2 * here), (me + d) % experts),
                slots.at[here, me],
                ex_ss.at[which, dx * experts + d],
                ex_rs.at[which, here * experts + me],
                beside(dx, d),
            )
            for dx, d in offsets
        ]

    def arrivals(slots, which):
        for dx, d in offsets:
            group, source = here + dx * (1 - 2 * here), (me + d) % experts
            remote(
                slots.at[group, source],
                slots.at[group, source],
                ex_ss.at[which, dx * experts + d],
                ex_rs.at[which, group * experts + source],
                beside(dx, d),
            ).wait_recv()

    half = lax.broadcasted_iota(jnp.int32, (tok, LANES), 1) < HEAD
    first = half.astype(bf16)
    second = (1.0 - half.astype(f32)).astype(bf16)

    def stack(value):
        return jnp.concatenate([value * first, value * second], 0)

    own_copies[2].wait()
    own_copies[3].wait()

    @pl.when(place > 0)
    def _():
        for copy in to_up:
            copy.wait_recv()

    for way in range(2):

        @pl.when(jnp.logical_not(comes[way]))
        def _():
            side_q[way] = jnp.zeros((tok, width), bf16)
            side_o[way] = jnp.zeros((tok, width), bf16)
            stat_recv[way] = jnp.zeros((2, heads, tok), f32)

    @pl.when(place == 0)
    def _():
        kx[pl.ds(0, REACH), :] = jnp.zeros((REACH, width), bf16)
        vx[pl.ds(0, REACH), :] = jnp.zeros((REACH, width), bf16)

    @pl.when(place < n - 1)
    def _():
        for copy in to_down:
            copy.wait_recv()

    @pl.when(place == n - 1)
    def _():
        kx[pl.ds(REACH + tok, REACH), :] = jnp.zeros((REACH, width), bf16)
        vx[pl.ds(REACH + tok, REACH), :] = jnp.zeros((REACH, width), bf16)

    sends_g = exchange(lambda group, expert: g_send.at[expert], g_slots, 0)
    for copy in sends_g:
        copy.start()
    own_copies[5].wait()

    if structured:

        def relay(k):
            owner = column(k) * 4 + low
            for j in range(2):
                landed(owner, j)

                @pl.when(middle)
                def _():
                    push(owner, j, 0, k, at(me, jnp.where(k == 1, far, near))).start()

                push(owner, j, 2, k, at(me, other_c)).start()

        relay(1)

        @pl.when(middle)
        def _():
            relay(2)

    def keep(kind, i, line):
        stats[kind] = jnp.where(
            lane == 2 * i, line[:tok], jnp.where(lane == 2 * i + 1, line[tok:], stats[kind])
        )

    def forward(i, carry):
        cols = pl.ds(pl.multiple_of(i * LANES, LANES), LANES)
        scores = dot(stack(queries[:, cols]), kx[:, cols], ((1,), (1,))) * HEAD ** (-0.5)
        both = jnp.concatenate([bias[...], bias[...]], 0)
        scores = scores + both
        top = jnp.max(scores, -1, keepdims=True)
        weight = jnp.exp(scores - top)
        total = jnp.sum(weight, -1, keepdims=True)
        prob = weight / total
        probs[i] = prob
        keep(0, i, top + jnp.log(total))
        mixed = dot(prob.astype(bf16), vx[:, cols], ((1,), (0,)))
        attn[:, cols] = jnp.where(half, mixed[:tok], mixed[tok:])
        return carry

    stats[...] = jnp.zeros_like(stats)
    lax.fori_loop(0, pairs, forward, 0)
    stat_send[0] = jnp.transpose(stats[0])[:heads]

    own_copies[6].wait()
    mid = acts[...].astype(f32) + attn[...]
    rms = lax.rsqrt(jnp.mean(mid * mid, -1, keepdims=True) + EPS)
    normed_s[...] = mid * rms
    inner = (normed_s[...] * gain[...]).astype(bf16)
    moved_u = dot(disp, inner, ((0,), (0,))).astype(bf16)
    u_send[...] = moved_u.reshape(experts, cap, width)
    u_slots[here, me] = u_send[me]
    sends_u = exchange(lambda group, expert: u_send.at[expert], u_slots, 1)
    for copy in sends_u:
        copy.start()
    late = (place == n - 5, place == 4) if structured else (False, False)
    tell((1,))
    for way in range(2):

        @pl.when(has[way] & jnp.logical_not(late[way]))
        def _():
            beside_copy(0, way).start()


    inner_f = inner.astype(f32)
    router_f = router[...].astype(f32)
    r_lane = lane
    logits = jnp.full((tok, LANES), NEG, f32)
    for e in range(experts):
        logits = jnp.where(lane == e, jnp.sum(inner_f * router_f[e : e + 1, :], -1, keepdims=True), logits)
    chance = jnp.exp(logits - jnp.max(logits, -1, keepdims=True))
    chance = chance / jnp.sum(chance, -1, keepdims=True)
    chosen = (route == r_lane).astype(f32)
    pick = jnp.sum(chance * chosen, -1, keepdims=True)

    own_copies[0].wait()
    own_copies[1].wait()
    inner_acc[...] = jnp.zeros_like(inner_acc)
    pick_acc[...] = jnp.zeros_like(pick_acc)
    per = max(1, 256 // frows)

    span_w = per * frows

    def first_half(start):
        wi = weights[pl.ds(start, per), 0].reshape(span_w, width)
        hidden = dot(u_slots[...].reshape(groups * rows, width), wi, ((1,), (1,)))
        square = hidden * hidden
        t = jnp.tanh(GELU_C * hidden * (1.0 + GELU_A * square))
        gate = 0.5 * (1.0 + t)
        act = (hidden * gate).astype(bf16).astype(f32)
        slope = gate + 0.5 * hidden * (1.0 - t * t) * (GELU_C * (1.0 + 3.0 * GELU_A * square))
        act_s[...] = act.reshape(groups, rows, span_w)
        slope_s[...] = slope.reshape(groups, rows, span_w)

    def second_half(start):
        wi = weights[pl.ds(start, per), 0].reshape(span_w, width)
        wo = weights[pl.ds(start, per), 1].reshape(span_w, width)
        back = dot(g_slots[...].reshape(groups * rows, width), wo, ((1,), (1,)))
        act = act_s[...].reshape(groups * rows, span_w)
        slope = slope_s[...].reshape(groups * rows, span_w)
        pick_acc[...] += jnp.sum(act * back, -1, keepdims=True).reshape(groups, rows, 1)
        inner_acc[...] += dot((back * slope).astype(bf16), wi, ((1,), (0,))).reshape(groups, rows, width)

    eye = (
        lax.broadcasted_iota(jnp.int32, (cap, LANES), 0) == lax.broadcasted_iota(jnp.int32, (cap, LANES), 1)
    ).astype(f32)

    def last_half(start, group):
        wi = weights[pl.ds(start, per), 0].reshape(span_w, width)
        wo = weights[pl.ds(start, per), 1].reshape(span_w, width)
        back = dot(g_slots[group].reshape(rows, width), wo, ((1,), (1,)))
        picked = pick_acc[group] + jnp.sum(act_s[group] * back, -1, keepdims=True)
        total = inner_acc[group] + dot((back * slope_s[group]).astype(bf16), wi, ((1,), (0,)))
        b_send[group] = total.astype(bf16).reshape(experts, cap, width)
        for e in range(experts):
            line = jnp.sum(picked[e * cap : (e + 1) * cap] * eye, 0, keepdims=True)
            p_send[group, e] = jnp.broadcast_to(line, (8, LANES))

    sends_b = exchange(lambda group, expert: b_send.at[group, expert], b_slots, 2)
    sends_p = exchange(lambda group, expert: p_send.at[group, expert], p_slots, 3)

    def give_back(wanted):
        for (dx, d), p_copy, b_copy in list(zip(offsets, sends_p, sends_b))[::-1]:
            if dx in wanted:
                p_copy.start()
                b_copy.start()

    if structured:

        @pl.when(middle)
        def _():
            relay(3)

        @pl.when(jnp.logical_not(middle))
        def _():
            relay(2)

        arrivals(g_slots, 0)
        arrivals(u_slots, 1)

        def step(k, carry):
            start = column(k) * 4 + x * 2
            landed(start + 1 - place % 2, 0)
            first_half(start)
            landed(start + 1 - place % 2, 1)
            second_half(start)
            return carry

        lax.fori_loop(0, 3, step, 0)

        @pl.when(jnp.logical_not(middle))
        def _():
            relay(3)

        start = column(3) * 4 + x * 2
        landed(start + 1 - place % 2, 0)
        first_half(start)
        landed(start + 1 - place % 2, 1)
    else:

        def settle(d, carry):
            for j in range(2):
                landed((place + d) % n, j)
            return carry

        lax.fori_loop(1, n, settle, 0)
        arrivals(g_slots, 0)
        arrivals(u_slots, 1)

        def step(j, carry):
            first_half(j * per)
            second_half(j * per)
            return carry

        lax.fori_loop(0, n // per - 1, step, 0)
        start = n - per
        first_half(start)

    for dx in range(groups)[::-1]:
        last_half(start, here + dx * (1 - 2 * here))
        give_back((dx,))

    hear((0, 1))

    def column_of(table, at_lane):
        return jnp.sum(jnp.where(lane == at_lane, table, 0.0), -1, keepdims=True)

    def upright(table):
        if table.shape[0] < tok:
            table = jnp.concatenate([table, jnp.zeros((tok - table.shape[0], tok), f32)], 0)
        return jnp.transpose(table)

    for way in range(2):
        stats[2 + way] = upright(stat_recv[way, 0])
    own = pl.ds(REACH, tok)

    def beside_probs(i, carry):
        cols = pl.ds(pl.multiple_of(i * LANES, LANES), LANES)
        for way in range(2):
            scores = dot(stack(side_q[way, :, cols]), kx[own, cols], ((1,), (1,))) * HEAD ** (-0.5)
            scores = scores + jnp.concatenate([side_bias[way], side_bias[way]], 0)
            line = jnp.concatenate([column_of(stats[2 + way], 2 * i), column_of(stats[2 + way], 2 * i + 1)], 0)
            side_probs[i, way * 2 * tok : (way + 1) * 2 * tok, :] = jnp.exp(scores - line)
        return carry

    lax.fori_loop(0, pairs, beside_probs, 0)

    b_slots[here, me] = b_send[here, me]
    p_slots[here, me] = p_send[here, me]
    arrivals(p_slots, 3)
    arrivals(b_slots, 2)

    normed = normed_s[...]
    part_inner = dot(disp, b_slots[0].reshape(rows, width), ((1,), (0,)))
    for group in range(1, groups):
        part_inner = part_inner + dot(disp, b_slots[group].reshape(rows, width), ((1,), (0,)))
    picks = jnp.zeros((tok, LANES), f32)
    for e in range(experts):
        line = p_slots[0, e, :1, :]
        for group in range(1, groups):
            line = line + p_slots[group, e, :1, :]
        picks = jnp.where(route == e, line, picks)
    grad_pick = jnp.sum(jnp.where(rank == lane, picks, 0.0), -1, keepdims=True)
    grad_logits = (grad_pick * pick) * (chosen - chance)
    grad_inner = pick * part_inner

    def pack(at_row, line):
        for c in range(pairs):
            where = at_row * pairs + c
            red_send[0, where : where + 1, :] = line[:, c * LANES : (c + 1) * LANES]

    inner_f = (normed * gain[...]).astype(bf16).astype(f32)
    for e in range(experts):
        column_e = grad_logits[:, e : e + 1]
        grad_inner = grad_inner + column_e * router_f[e : e + 1, :]
        pack(e, jnp.sum(inner_f * column_e, 0, keepdims=True))
    pack(experts, jnp.sum(grad_inner * normed, 0, keepdims=True))
    grad_normed = grad_inner * gain[...]
    grad_mid = rms * (
        grad_normed - normed * jnp.mean(grad_normed * normed, -1, keepdims=True)
    ) + grad_out[...].astype(f32)
    grad_acts[...] = grad_mid.astype(bf16)
    results = [
        pltpu.make_async_copy(source, target, out_sem.at[i])
        for i, (source, target) in enumerate(
            ((grad_acts, grad_acts_h), (grad_q, grad_q_h), (grad_k, grad_k_h), (grad_v, grad_v_h))
        )
    ]
    results[0].start()
    for way in range(2):

        @pl.when(has[way] & late[way])
        def _():
            beside_copy(0, way).start()

    tell((4,))

    reduces = [
        [
            remote(red_send.at[j], red_recv.at[j, i], red_ss.at[j, i], red_rs.at[j, i], at(flip(me, e), flip(place, m)))
            for i, (e, m) in enumerate(masks)
        ]
        for j, masks in enumerate(rounds)
    ]

    def reduce_step(j):
        total = red_send[j]
        for i, copy in enumerate(reduces[j]):
            copy.wait_recv()
            total = total + red_recv[j, i]
        if j + 1 < len(reduces):
            red_send[j + 1] = total
            for copy in reduces[j + 1]:
                copy.start()
        else:
            small_out[...] = total

    for copy in reduces[0]:
        copy.start()

    def backward(i, carry):
        for j in range(len(reduces) - 1):

            @pl.when(i == pairs // 2 + j)
            def _():
                reduce_step(j)

        cols = pl.ds(pl.multiple_of(i * LANES, LANES), LANES)
        o_stack = stack(grad_acts[:, cols])
        q_stack = stack(queries[:, cols])
        prob = probs[i]
        grad_probs = dot(o_stack, vx[:, cols], ((1,), (1,)))
        own_value = dot(prob[:, REACH : REACH + tok].astype(bf16), o_stack, ((0,), (0,)))
        delta = jnp.sum(prob * grad_probs, -1, keepdims=True)
        keep(1, i, delta)
        grad_scores = (prob * (grad_probs - delta) * HEAD ** (-0.5)).astype(bf16)
        query_terms = dot(grad_scores, kx[:, cols], ((1,), (0,)))
        grad_q[:, cols] = jnp.where(half, query_terms[:tok], query_terms[tok:]).astype(bf16)
        own_key = dot(grad_scores[:, REACH : REACH + tok], q_stack, ((0,), (0,)))
        own_kv[0, :, cols] = own_key
        own_kv[1, :, cols] = own_value
        return carry

    for t in range(2):
        lax.fori_loop(t * (pairs // 2), (t + 1) * (pairs // 2), backward, 0)
        stat_send[1, half_rows(t)] = jnp.transpose(stats[1])[t * pairs : (t + 1) * pairs]
        tell((2, 5) if t == 0 else (3,))
    results[1].start()

    def finish(t, i, carry):
        cols = pl.ds(pl.multiple_of(i * LANES, LANES), LANES)
        o_all = jnp.concatenate([stack(side_o[way, :, cols]) for way in range(2)], 0)
        q_all = jnp.concatenate([stack(side_q[way, :, cols]) for way in range(2)], 0)
        prob = side_probs[i]
        line = jnp.concatenate(
            [column_of(stats[2 + way], 2 * i + h - t * pairs) for way in range(2) for h in range(2)], 0
        )
        grad_probs = dot(o_all, vx[own, cols], ((1,), (1,)))
        grad_scores = (prob * (grad_probs - line) * HEAD ** (-0.5)).astype(bf16)
        grad_k[:, cols] = (own_kv[0, :, cols] + dot(grad_scores, q_all, ((0,), (0,)))).astype(bf16)
        grad_v[:, cols] = (own_kv[1, :, cols] + dot(prob.astype(bf16), o_all, ((0,), (0,)))).astype(bf16)
        return carry

    for t in range(2):
        hear((2 + t, 4 + t))
        for way in range(2):
            stats[2 + way] = upright(stat_recv[way, 1, t * pairs : (t + 1) * pairs])
        lax.fori_loop(t * (pairs // 2), (t + 1) * (pairs // 2), functools.partial(finish, t), 0)
    results[2].start()
    results[3].start()
    reduce_step(len(reduces) - 1)

    @pl.when(place < n - 1)
    def _():
        for copy in to_up:
            copy.wait_send()

    @pl.when(place > 0)
    def _():
        for copy in to_down:
            copy.wait_send()

    for copy in sends_g + sends_u + sends_b + sends_p + [c for group in reduces for c in group]:
        copy.wait_send()

    for way in range(2):

        @pl.when(has[way])
        def _():
            for kind in range(6):
                beside_copy(kind, way).wait_send()

    if structured:
        for j in range(2):
            push(place, j, 0, 0, at(me, near), mine[j]).wait_send()

        @pl.when(middle)
        def _():
            for j in range(2):
                push(place, j, 1, 0, at(me, far), mine[j]).wait_send()

        def sent(k, carry):
            for j in range(2):

                @pl.when((k > 0) & middle)
                def _():
                    push(place, j, 0, k, at(me, near)).wait_send()

                push(place, j, 2, k, at(me, near)).wait_send()
            return carry

        lax.fori_loop(0, 4, sent, 0)
    else:

        def sent(d, carry):
            for j in range(2):
                push(place, j, 0, d, at(me, (place + d) % n), mine[j]).wait_send()
            return carry

        lax.fori_loop(1, n, sent, 0)
    for copy in results:
        copy.wait()


def shards(acts, queries, keys, values, grad_out, gain, router, w_in, w_out, routes, tissue):
    tok, width = acts.shape[1:]
    n = lax.axis_size("seq")
    experts = router.shape[1]
    cap = max(2, 5 * tok // (4 * experts))
    cap = -(-cap // 16) * 16
    rows = experts * cap
    frows = w_in.shape[1]
    span = tok + 2 * REACH
    pairs = width // LANES
    lines = (experts + 1) * pairs
    per = max(1, 256 // frows)
    rounds = reduce_rounds(n, experts)
    most = max(len(masks) for masks in rounds)
    groups = 2 if n == 16 else 1
    bf16, f32 = jnp.bfloat16, jnp.float32
    vmem = pl.BlockSpec(memory_space=pltpu.VMEM)
    hbm = pl.BlockSpec(memory_space=pl.ANY)
    big = jax.ShapeDtypeStruct((tok, width), bf16)
    dma = pltpu.SemaphoreType.DMA
    steps = 4 if n == 16 else n
    outs = pl.pallas_call(
        functools.partial(kernel, n, experts, cap, tissue.shape[1], groups),
        out_shape=[big, big, big, big, jax.ShapeDtypeStruct((lines, LANES), f32)],
        in_specs=[hbm] * 5 + [vmem] * 2 + [hbm] * 2 + [vmem, pl.BlockSpec(memory_space=pltpu.SMEM)],
        out_specs=[hbm] * 4 + [vmem],
        scratch_shapes=[pltpu.VMEM((tok, width), bf16)] * 7
        + [pltpu.VMEM((groups, rows, per * frows), f32)] * 2
        + [
            pltpu.VMEM((n, 2, frows, width), bf16),
            pltpu.VMEM((span, width), bf16),
            pltpu.VMEM((span, width), bf16),
            pltpu.VMEM((tok, span), f32),
            pltpu.VMEM((pairs, 2 * tok, span), f32),
            pltpu.VMEM((tok, width), f32),
            pltpu.VMEM((tok, width), f32),
            pltpu.VMEM((experts, cap, width), bf16),
            pltpu.VMEM((groups, experts, cap, width), bf16),
            pltpu.VMEM((experts, cap, width), bf16),
            pltpu.VMEM((groups, experts, cap, width), bf16),
            pltpu.VMEM((groups, rows, width), f32),
            pltpu.VMEM((groups, rows, 1), f32),
            pltpu.VMEM((groups, experts, cap, width), bf16),
            pltpu.VMEM((groups, experts, cap, width), bf16),
            pltpu.VMEM((groups, experts, 8, LANES), f32),
            pltpu.VMEM((groups, experts, 8, LANES), f32),
            pltpu.VMEM((2, tok, width), f32),
            pltpu.VMEM((4, tok, LANES), f32),
            pltpu.VMEM((2, 2 * pairs, tok), f32),
            pltpu.VMEM((2, 2, 2 * pairs, tok), f32),
            pltpu.VMEM((2, tok, tok), f32),
            pltpu.VMEM((2, tok, width), bf16),
            pltpu.VMEM((2, tok, width), bf16),
            pltpu.VMEM((pairs, 4 * tok, tok), f32),
            pltpu.VMEM((len(rounds), lines, LANES), f32),
            pltpu.VMEM((len(rounds), most, lines, LANES), f32),
            dma((7,)),
            dma((4,)),
            dma((2, 2)),
            dma((2, 2)),
            dma((3, steps, 2)),
            dma((n, 2)),
            dma((4, groups * experts)),
            dma((4, groups * experts)),
            dma((6, 2)),
            dma((6, 2)),
            dma((len(rounds), most)),
            dma((len(rounds), most)),
        ],
        compiler_params=pltpu.CompilerParams(
            collective_id=0, has_side_effects=True, vmem_limit_bytes=60 * 1024 * 1024
        ),
    )(
        acts[0], queries[0], keys[0], values[0], grad_out[0], gain[None], router.T,
        w_in[0], w_out[0], routes[:, :, 0], tissue,
    )
    outs = pl.pallas_call(
        hand_out,
        out_shape=[
            big, big, big, big,
            jax.ShapeDtypeStruct((experts, width), f32), jax.ShapeDtypeStruct((1, width), f32),
        ],
        in_specs=[vmem] * 5,
        out_specs=[vmem] * 6,
    )(*outs)
    return tuple(out[None] for out in outs[:4]) + (outs[4].T, outs[5][0])


def hand_out(*refs):
    for source, target in zip(refs[:4], refs[5:9]):
        target[...] = source[...]
    small, experts = refs[4], refs[9].shape[0]
    pairs = small.shape[0] // (experts + 1)
    for row in range(experts + 1):
        target, line = (refs[9], row) if row < experts else (refs[10], 0)
        for c in range(pairs):
            where = row * pairs + c
            target[line : line + 1, c * LANES : (c + 1) * LANES] = small[where : where + 1, :]


def solution(mesh):
    tiles = P("expert", "seq", None)
    in_specs = (tiles,) * 5 + (P(), P()) + (tiles,) * 3 + (P("expert", None),)
    out_specs = (tiles,) * 4 + (P(), P())
    return jax.shard_map(shards, mesh=mesh, in_specs=in_specs, out_specs=out_specs, check_vma=False)
```

```python
import functools

import jax
import jax.numpy as jnp
from jax import lax
from jax.experimental import pallas as pl
from jax.experimental.pallas import tpu as pltpu
from jax.sharding import PartitionSpec as P

HEAD = 64
REACH = 128
BLOCK = 512
EPS = 1e-06
LANES = 128
NEG = -1e30
GELU_C = 0.7978845608028654
GELU_A = 0.044715
MESH = pl.DeviceIdType.MESH


def dot(a, b, contract, precision=None):
    return lax.dot_general(
        a, b, (contract, ((), ())), preferred_element_type=jnp.float32, precision=precision
    )


def flip(index, mask):
    size = 1
    while size <= mask:
        if mask & size:
            index = index + size - 2 * size * ((index // size) % 2)
        size *= 2
    return index


def reduce_rounds(n, experts):
    bits = [(1 << b, 0) for b in range((experts - 1).bit_length())]
    bits += [(0, 1 << b) for b in range((n - 1).bit_length())]
    rounds = []
    for start in range(0, len(bits), 3):
        masks = [(0, 0)]
        for e, m in bits[start : start + 3]:
            masks += [(a + e, b + m) for a, b in masks]
        rounds.append(masks[1:])
    return rounds


def kernel(
    n, experts, cap, nblocks, groups,
    acts_h, queries_h, keys, values, grad_out_h, gain, router, w_in, w_out, routes, tissue,
    grad_acts_h, grad_q_h, grad_k_h, grad_v_h, small_out,
    acts, queries, grad_out, grad_acts, grad_q, grad_k, grad_v, act_s, slope_s,
    weights, kx, vx, bias, probs, attn, normed_s, u_send, u_slots, g_send, g_slots,
    inner_acc, pick_acc, b_send, b_slots, p_send, p_slots, own_kv,
    stats, stat_send, stat_recv, side_bias, side_q, side_o, side_probs, relay_v, red_send, red_recv,
    local_sem, out_sem, halo_ss, halo_rs, w_ss, w_rs, ex_ss, ex_rs, nb_ss, nb_rs, relay_sem, red_ss, red_rs,
):
    tok, width = acts_h.shape
    span = tok + 2 * REACH
    frows = w_in.shape[0]
    rows = experts * cap
    pairs = width // LANES
    place = lax.axis_index("seq")
    me = lax.axis_index("expert")
    structured = n == 16
    bf16, f32 = jnp.bfloat16, jnp.float32

    def at(expert, seq):
        return (expert, seq)

    def remote(src, dst, ss, rs, where):
        return pltpu.make_async_remote_copy(
            src_ref=src, dst_ref=dst, send_sem=ss, recv_sem=rs, device_id=where, device_id_type=MESH
        )

    barrier = pltpu.get_barrier_semaphore()
    rounds = reduce_rounds(n, experts)
    peers = [at(flip(me, e), flip(place, m)) for masks in rounds for e, m in masks]
    if structured:
        z = place // 4
        peers += [at(me, (place + d) % n) for d in (1, n - 1, 3, n - 3)]
    else:
        peers += [at(me, (place + d) % n) for d in range(1, n)]
        peers += [at((me + d) % experts, place) for d in range(1, experts)]
    for peer in peers:
        pl.semaphore_signal(barrier, inc=1, device_id=peer, device_id_type=MESH)

    own_copies = [
        pltpu.make_async_copy(w_in, weights.at[place, 0], local_sem.at[0]),
        pltpu.make_async_copy(w_out, weights.at[place, 1], local_sem.at[1]),
        pltpu.make_async_copy(keys, kx.at[pl.ds(REACH, tok)], local_sem.at[2]),
        pltpu.make_async_copy(values, vx.at[pl.ds(REACH, tok)], local_sem.at[3]),
        pltpu.make_async_copy(grad_out_h, grad_out, local_sem.at[4]),
        pltpu.make_async_copy(queries_h, queries, local_sem.at[5]),
        pltpu.make_async_copy(acts_h, acts, local_sem.at[6]),
    ]
    for copy in own_copies:
        copy.start()
    lane = lax.broadcasted_iota(jnp.int32, (tok, LANES), 1)
    row_at = lax.broadcasted_iota(jnp.int32, (tok, tok), 0)
    col_at = lax.broadcasted_iota(jnp.int32, (tok, tok), 1)
    spread_routes = jnp.where(row_at == col_at, jnp.broadcast_to(routes[...], (tok, tok)), 0)
    route = jnp.sum(spread_routes.astype(f32), -1, keepdims=True).astype(jnp.int32)
    onehot = (route == lane).astype(f32)
    lower = (row_at > col_at).astype(bf16)
    before = dot(lower, onehot.astype(bf16), ((1,), (0,)))
    rank = jnp.sum(before * onehot, -1, keepdims=True).astype(jnp.int32)
    slot = route * cap + rank
    disp = (slot == lax.broadcasted_iota(jnp.int32, (tok, rows), 1)).astype(bf16)

    here = (place // 2) % 2 if structured else 0
    q_at = place * tok + lax.broadcasted_iota(jnp.int32, (tok, span), 0)
    k_at = place * tok - REACH + lax.broadcasted_iota(jnp.int32, (tok, span), 1)
    live = jnp.zeros((tok, span), jnp.int32)
    for b in range(nblocks):
        live = jnp.where((k_at >= b * BLOCK) & (k_at < (b + 1) * BLOCK), tissue[0, b], live)
    near_by = jnp.abs(q_at - k_at) <= REACH
    allow = near_by & (k_at >= 0) & (k_at < n * tok) & ((live == 1) | (q_at == k_at))
    bias[...] = jnp.where(allow, 0.0, NEG).astype(f32)
    live_own = live[:, REACH : REACH + tok] == 1
    for r, near_side in enumerate(((col_at <= row_at) & (place > 0), (row_at <= col_at) & (place < n - 1))):
        side_bias[r] = jnp.where(near_side & live_own, 0.0, NEG).astype(f32)
    own_copies[4].wait()
    moved_g = dot(disp, grad_out[...], ((0,), (0,))).astype(bf16)
    g_send[...] = moved_g.reshape(experts, cap, width)
    g_slots[here, me] = g_send[me]
    pl.semaphore_wait(barrier, len(peers))

    up, down = at(me, (place + 1) % n), at(me, (place + n - 1) % n)
    to_up = [
        remote(src, dst.at[pl.ds(0, REACH)], halo_ss.at[i, 0], halo_rs.at[i, 0], up)
        for i, (src, dst) in enumerate(((keys, kx), (values, vx)))
    ]
    to_down = [
        remote(src, dst.at[pl.ds(REACH + tok, REACH)], halo_ss.at[i, 1], halo_rs.at[i, 1], down)
        for i, (src, dst) in enumerate(((keys, kx), (values, vx)))
    ]

    heads = 2 * pairs
    targets = (up, down)
    has = (place < n - 1, place > 0)
    comes = (place > 0, place < n - 1)

    def half_rows(t):
        return pl.ds(t * pairs, pairs)

    def half_cols(t):
        return pl.ds(t * (width // 2), width // 2)

    def beside_copy(kind, way):
        if kind == 0:
            src, dst = queries_h, side_q.at[way]
        elif kind == 1:
            src, dst = stat_send.at[0], stat_recv.at[way, 0]
        elif kind < 4:
            src, dst = (stat_send.at[1, half_rows(kind - 2)], stat_recv.at[way, 1, half_rows(kind - 2)])
        else:
            src, dst = grad_acts.at[:, half_cols(kind - 4)], side_o.at[way, :, half_cols(kind - 4)]
        return remote(src, dst, nb_ss.at[kind, way], nb_rs.at[kind, way], targets[way])

    def tell(kinds, ways=(0, 1)):
        for way in ways:

            @pl.when(has[way])
            def _():
                for kind in kinds:
                    beside_copy(kind, way).start()

    def hear(kinds):
        for way in range(2):

            @pl.when(comes[way])
            def _():
                for kind in kinds:
                    beside_copy(kind, way).wait_recv()

    if structured:
        seat = place % 4
        over = (
            remote(values, relay_v, halo_ss.at[1, 0], relay_sem.at[0], at(me, (place + n - 2) % n)),
            remote(values, relay_v, halo_ss.at[1, 1], relay_sem.at[0], at(me, (place + 2) % n)),
        )
        onward = (
            remote(relay_v, vx.at[pl.ds(0, REACH)], relay_sem.at[1], halo_rs.at[1, 0], at(me, (place + 3) % n)),
            remote(
                relay_v, vx.at[pl.ds(REACH + tok, REACH)], relay_sem.at[1], halo_rs.at[1, 1], at(me, (place + n - 3) % n)
            ),
        )
        turns = ((seat == 1) & (place < n - 3), (seat == 2) & (place > 2))
        aside = (seat == 3, seat == 0)
    else:
        aside = (False, False)

    for way, copies in enumerate((to_up, to_down)):

        @pl.when(has[way])
        def _():
            copies[0].start()

        @pl.when(has[way] & jnp.logical_not(aside[way]))
        def _():
            copies[1].start()

        if structured:

            @pl.when(has[way] & aside[way])
            def _():
                over[way].start()

    def push(owner, j, kind, step, where, src=None):
        return remote(
            weights.at[owner, j] if src is None else src,
            weights.at[owner, j],
            w_ss.at[kind, step, j],
            w_rs.at[owner, j],
            where,
        )

    def landed(owner, j):
        push(owner, j, 0, 0, up).wait_recv()

    mine = (w_in, w_out)
    if structured:
        x = (place // 2) % 2
        low = place % 4
        middle = (z == 1) | (z == 2)
        near, far = flip(place, 4), flip(place, 12)
        other_c = flip(place, 1)

        def column(k):
            return jnp.where(
                k == 0, z, jnp.where(k == 1, z + 1 - 2 * (z % 2), jnp.where(k == 2, 2 - z // 2, 3 - 3 * (z // 2)))
            )

        for j in range(2):
            push(place, j, 0, 0, at(me, near), mine[j]).start()

        @pl.when(middle)
        def _():
            for j in range(2):
                push(place, j, 1, 0, at(me, far), mine[j]).start()

        for j in range(2):
            push(place, j, 2, 0, at(me, other_c), mine[j]).start()
    else:

        def spread(d, carry):
            for j in range(2):
                push(place, j, 0, d, at(me, (place + d) % n), mine[j]).start()
            return carry

        lax.fori_loop(1, n, spread, 0)

    offsets = [(dx, d) for dx in range(groups) for d in range(experts)][1:]

    def beside(dx, d):
        return at((me + d) % experts, flip(place, 2 * dx))

    def exchange(piece, slots, which):
        return [
            remote(
                piece(here + dx * (1 - 2 * here), (me + d) % experts),
                slots.at[here, me],
                ex_ss.at[which, dx * experts + d],
                ex_rs.at[which, here * experts + me],
                beside(dx, d),
            )
            for dx, d in offsets
        ]

    def arrivals(slots, which):
        for dx, d in offsets:
            group, source = here + dx * (1 - 2 * here), (me + d) % experts
            remote(
                slots.at[group, source],
                slots.at[group, source],
                ex_ss.at[which, dx * experts + d],
                ex_rs.at[which, group * experts + source],
                beside(dx, d),
            ).wait_recv()

    half = lax.broadcasted_iota(jnp.int32, (tok, LANES), 1) < HEAD
    first = half.astype(bf16)
    second = (1.0 - half.astype(f32)).astype(bf16)

    def stack(value):
        return jnp.concatenate([value * first, value * second], 0)

    own_copies[2].wait()
    own_copies[3].wait()
    if structured:
        for way in range(2):

            @pl.when(turns[way])
            def _():
                over[way].wait_recv()
                onward[way].start()

    @pl.when(place > 0)
    def _():
        for copy in to_up:
            copy.wait_recv()

    for way in range(2):

        @pl.when(jnp.logical_not(comes[way]))
        def _():
            side_q[way] = jnp.zeros((tok, width), bf16)
            side_o[way] = jnp.zeros((tok, width), bf16)
            stat_recv[way] = jnp.zeros((2, heads, tok), f32)

    @pl.when(place == 0)
    def _():
        kx[pl.ds(0, REACH), :] = jnp.zeros((REACH, width), bf16)
        vx[pl.ds(0, REACH), :] = jnp.zeros((REACH, width), bf16)

    @pl.when(place < n - 1)
    def _():
        for copy in to_down:
            copy.wait_recv()

    @pl.when(place == n - 1)
    def _():
        kx[pl.ds(REACH + tok, REACH), :] = jnp.zeros((REACH, width), bf16)
        vx[pl.ds(REACH + tok, REACH), :] = jnp.zeros((REACH, width), bf16)

    sends_g = exchange(lambda group, expert: g_send.at[expert], g_slots, 0)
    for copy in sends_g:
        copy.start()
    own_copies[5].wait()

    if structured:

        def relay(k):
            owner = column(k) * 4 + low
            for j in range(2):
                landed(owner, j)

                @pl.when(middle)
                def _():
                    push(owner, j, 0, k, at(me, jnp.where(k == 1, far, near))).start()

                push(owner, j, 2, k, at(me, other_c)).start()

        relay(1)

        @pl.when(middle)
        def _():
            relay(2)

    def keep(kind, i, line):
        stats[kind] = jnp.where(
            lane == 2 * i, line[:tok], jnp.where(lane == 2 * i + 1, line[tok:], stats[kind])
        )

    def forward(i, carry):
        cols = pl.ds(pl.multiple_of(i * LANES, LANES), LANES)
        scores = dot(stack(queries[:, cols]), kx[:, cols], ((1,), (1,))) * HEAD ** (-0.5)
        both = jnp.concatenate([bias[...], bias[...]], 0)
        scores = scores + both
        top = jnp.max(scores, -1, keepdims=True)
        weight = jnp.exp(scores - top)
        total = jnp.sum(weight, -1, keepdims=True)
        prob = weight / total
        probs[i] = prob
        keep(0, i, top + jnp.log(total))
        mixed = dot(prob.astype(bf16), vx[:, cols], ((1,), (0,)))
        attn[:, cols] = jnp.where(half, mixed[:tok], mixed[tok:])
        return carry

    stats[...] = jnp.zeros_like(stats)
    lax.fori_loop(0, pairs, forward, 0)
    stat_send[0] = jnp.transpose(stats[0])[:heads]

    own_copies[6].wait()
    mid = acts[...].astype(f32) + attn[...]
    rms = lax.rsqrt(jnp.mean(mid * mid, -1, keepdims=True) + EPS)
    normed_s[...] = mid * rms
    inner = (normed_s[...] * gain[...]).astype(bf16)
    moved_u = dot(disp, inner, ((0,), (0,))).astype(bf16)
    u_send[...] = moved_u.reshape(experts, cap, width)
    u_slots[here, me] = u_send[me]
    sends_u = exchange(lambda group, expert: u_send.at[expert], u_slots, 1)
    for copy in sends_u:
        copy.start()
    late = (place == n - 5, place == 4) if structured else (False, False)
    tell((1,))
    for way in range(2):

        @pl.when(has[way] & jnp.logical_not(late[way]))
        def _():
            beside_copy(0, way).start()


    inner_f = inner.astype(f32)
    router_f = router[...].astype(f32)
    r_lane = lane
    logits = jnp.full((tok, LANES), NEG, f32)
    for e in range(experts):
        logits = jnp.where(lane == e, jnp.sum(inner_f * router_f[e : e + 1, :], -1, keepdims=True), logits)
    chance = jnp.exp(logits - jnp.max(logits, -1, keepdims=True))
    chance = chance / jnp.sum(chance, -1, keepdims=True)
    chosen = (route == r_lane).astype(f32)
    pick = jnp.sum(chance * chosen, -1, keepdims=True)

    own_copies[0].wait()
    own_copies[1].wait()
    inner_acc[...] = jnp.zeros_like(inner_acc)
    pick_acc[...] = jnp.zeros_like(pick_acc)
    per = max(1, 256 // frows)

    span_w = per * frows

    def first_half(start):
        wi = weights[pl.ds(start, per), 0].reshape(span_w, width)
        hidden = dot(u_slots[...].reshape(groups * rows, width), wi, ((1,), (1,)))
        square = hidden * hidden
        t = jnp.tanh(GELU_C * hidden * (1.0 + GELU_A * square))
        gate = 0.5 * (1.0 + t)
        act = (hidden * gate).astype(bf16).astype(f32)
        slope = gate + 0.5 * hidden * (1.0 - t * t) * (GELU_C * (1.0 + 3.0 * GELU_A * square))
        act_s[...] = act.reshape(groups, rows, span_w)
        slope_s[...] = slope.reshape(groups, rows, span_w)

    def second_half(start):
        wi = weights[pl.ds(start, per), 0].reshape(span_w, width)
        wo = weights[pl.ds(start, per), 1].reshape(span_w, width)
        back = dot(g_slots[...].reshape(groups * rows, width), wo, ((1,), (1,)))
        act = act_s[...].reshape(groups * rows, span_w)
        slope = slope_s[...].reshape(groups * rows, span_w)
        pick_acc[...] += jnp.sum(act * back, -1, keepdims=True).reshape(groups, rows, 1)
        inner_acc[...] += dot((back * slope).astype(bf16), wi, ((1,), (0,))).reshape(groups, rows, width)

    eye = (
        lax.broadcasted_iota(jnp.int32, (cap, LANES), 0) == lax.broadcasted_iota(jnp.int32, (cap, LANES), 1)
    ).astype(f32)

    def last_half(start, group):
        wi = weights[pl.ds(start, per), 0].reshape(span_w, width)
        wo = weights[pl.ds(start, per), 1].reshape(span_w, width)
        back = dot(g_slots[group].reshape(rows, width), wo, ((1,), (1,)))
        picked = pick_acc[group] + jnp.sum(act_s[group] * back, -1, keepdims=True)
        total = inner_acc[group] + dot((back * slope_s[group]).astype(bf16), wi, ((1,), (0,)))
        b_send[group] = total.astype(bf16).reshape(experts, cap, width)
        for e in range(experts):
            line = jnp.sum(picked[e * cap : (e + 1) * cap] * eye, 0, keepdims=True)
            p_send[group, e] = jnp.broadcast_to(line, (8, LANES))

    sends_b = exchange(lambda group, expert: b_send.at[group, expert], b_slots, 2)
    sends_p = exchange(lambda group, expert: p_send.at[group, expert], p_slots, 3)

    def give_back(wanted):
        for (dx, d), p_copy, b_copy in list(zip(offsets, sends_p, sends_b))[::-1]:
            if dx in wanted:
                p_copy.start()
                b_copy.start()

    if structured:

        @pl.when(middle)
        def _():
            relay(3)

        @pl.when(jnp.logical_not(middle))
        def _():
            relay(2)

        arrivals(g_slots, 0)
        arrivals(u_slots, 1)

        def step(k, carry):
            start = column(k) * 4 + x * 2
            landed(start + 1 - place % 2, 0)
            first_half(start)
            landed(start + 1 - place % 2, 1)
            second_half(start)
            return carry

        lax.fori_loop(0, 3, step, 0)

        @pl.when(jnp.logical_not(middle))
        def _():
            relay(3)

        start = column(3) * 4 + x * 2
        landed(start + 1 - place % 2, 0)
        first_half(start)
        landed(start + 1 - place % 2, 1)
    else:

        def settle(d, carry):
            for j in range(2):
                landed((place + d) % n, j)
            return carry

        lax.fori_loop(1, n, settle, 0)
        arrivals(g_slots, 0)
        arrivals(u_slots, 1)

        def step(j, carry):
            first_half(j * per)
            second_half(j * per)
            return carry

        lax.fori_loop(0, n // per - 1, step, 0)
        start = n - per
        first_half(start)

    for dx in range(groups)[::-1]:
        last_half(start, here + dx * (1 - 2 * here))
        give_back((dx,))

    for way in range(2):

        @pl.when(has[way] & late[way])
        def _():
            beside_copy(0, way).start()

    hear((0, 1))

    def column_of(table, at_lane):
        return jnp.sum(jnp.where(lane == at_lane, table, 0.0), -1, keepdims=True)

    def upright(table):
        if table.shape[0] < tok:
            table = jnp.concatenate([table, jnp.zeros((tok - table.shape[0], tok), f32)], 0)
        return jnp.transpose(table)

    for way in range(2):
        stats[2 + way] = upright(stat_recv[way, 0])
    own = pl.ds(REACH, tok)

    def beside_probs(i, carry):
        cols = pl.ds(pl.multiple_of(i * LANES, LANES), LANES)
        for way in range(2):
            scores = dot(stack(side_q[way, :, cols]), kx[own, cols], ((1,), (1,))) * HEAD ** (-0.5)
            scores = scores + jnp.concatenate([side_bias[way], side_bias[way]], 0)
            line = jnp.concatenate([column_of(stats[2 + way], 2 * i), column_of(stats[2 + way], 2 * i + 1)], 0)
            side_probs[i, way * 2 * tok : (way + 1) * 2 * tok, :] = jnp.exp(scores - line)
        return carry

    lax.fori_loop(0, pairs, beside_probs, 0)

    b_slots[here, me] = b_send[here, me]
    p_slots[here, me] = p_send[here, me]
    arrivals(p_slots, 3)
    arrivals(b_slots, 2)

    normed = normed_s[...]
    part_inner = dot(disp, b_slots[0].reshape(rows, width), ((1,), (0,)))
    for group in range(1, groups):
        part_inner = part_inner + dot(disp, b_slots[group].reshape(rows, width), ((1,), (0,)))
    picks = jnp.zeros((tok, LANES), f32)
    for e in range(experts):
        line = p_slots[0, e, :1, :]
        for group in range(1, groups):
            line = line + p_slots[group, e, :1, :]
        picks = jnp.where(route == e, line, picks)
    grad_pick = jnp.sum(jnp.where(rank == lane, picks, 0.0), -1, keepdims=True)
    grad_logits = (grad_pick * pick) * (chosen - chance)
    grad_inner = pick * part_inner

    def pack(at_row, line):
        for c in range(pairs):
            where = at_row * pairs + c
            red_send[0, where : where + 1, :] = line[:, c * LANES : (c + 1) * LANES]

    inner_f = (normed * gain[...]).astype(bf16).astype(f32)
    for e in range(experts):
        column_e = grad_logits[:, e : e + 1]
        grad_inner = grad_inner + column_e * router_f[e : e + 1, :]
        pack(e, jnp.sum(inner_f * column_e, 0, keepdims=True))
    pack(experts, jnp.sum(grad_inner * normed, 0, keepdims=True))
    grad_normed = grad_inner * gain[...]
    grad_mid = rms * (
        grad_normed - normed * jnp.mean(grad_normed * normed, -1, keepdims=True)
    ) + grad_out[...].astype(f32)
    grad_acts[...] = grad_mid.astype(bf16)
    results = [
        pltpu.make_async_copy(source, target, out_sem.at[i])
        for i, (source, target) in enumerate(
            ((grad_acts, grad_acts_h), (grad_q, grad_q_h), (grad_k, grad_k_h), (grad_v, grad_v_h))
        )
    ]
    results[0].start()
    tell((4,))

    reduces = [
        [
            remote(red_send.at[j], red_recv.at[j, i], red_ss.at[j, i], red_rs.at[j, i], at(flip(me, e), flip(place, m)))
            for i, (e, m) in enumerate(masks)
        ]
        for j, masks in enumerate(rounds)
    ]

    def reduce_step(j):
        total = red_send[j]
        for i, copy in enumerate(reduces[j]):
            copy.wait_recv()
            total = total + red_recv[j, i]
        if j + 1 < len(reduces):
            red_send[j + 1] = total
            for copy in reduces[j + 1]:
                copy.start()
        else:
            small_out[...] = total

    for copy in reduces[0]:
        copy.start()

    def backward(i, carry):
        for j in range(len(reduces) - 1):

            @pl.when(i == pairs // 2 + j)
            def _():
                reduce_step(j)

        cols = pl.ds(pl.multiple_of(i * LANES, LANES), LANES)
        o_stack = stack(grad_acts[:, cols])
        q_stack = stack(queries[:, cols])
        prob = probs[i]
        grad_probs = dot(o_stack, vx[:, cols], ((1,), (1,)))
        own_value = dot(prob[:, REACH : REACH + tok].astype(bf16), o_stack, ((0,), (0,)))
        delta = jnp.sum(prob * grad_probs, -1, keepdims=True)
        keep(1, i, delta)
        grad_scores = (prob * (grad_probs - delta) * HEAD ** (-0.5)).astype(bf16)
        query_terms = dot(grad_scores, kx[:, cols], ((1,), (0,)))
        grad_q[:, cols] = jnp.where(half, query_terms[:tok], query_terms[tok:]).astype(bf16)
        own_key = dot(grad_scores[:, REACH : REACH + tok], q_stack, ((0,), (0,)))
        own_kv[0, :, cols] = own_key
        own_kv[1, :, cols] = own_value
        return carry

    for t in range(2):
        lax.fori_loop(t * (pairs // 2), (t + 1) * (pairs // 2), backward, 0)
        stat_send[1, half_rows(t)] = jnp.transpose(stats[1])[t * pairs : (t + 1) * pairs]
        tell((2, 5) if t == 0 else (3,))
    results[1].start()

    def finish(t, i, carry):
        cols = pl.ds(pl.multiple_of(i * LANES, LANES), LANES)
        o_all = jnp.concatenate([stack(side_o[way, :, cols]) for way in range(2)], 0)
        q_all = jnp.concatenate([stack(side_q[way, :, cols]) for way in range(2)], 0)
        prob = side_probs[i]
        line = jnp.concatenate(
            [column_of(stats[2 + way], 2 * i + h - t * pairs) for way in range(2) for h in range(2)], 0
        )
        grad_probs = dot(o_all, vx[own, cols], ((1,), (1,)))
        grad_scores = (prob * (grad_probs - line) * HEAD ** (-0.5)).astype(bf16)
        grad_k[:, cols] = (own_kv[0, :, cols] + dot(grad_scores, q_all, ((0,), (0,)))).astype(bf16)
        grad_v[:, cols] = (own_kv[1, :, cols] + dot(prob.astype(bf16), o_all, ((0,), (0,)))).astype(bf16)
        return carry

    for t in range(2):
        hear((2 + t, 4 + t))
        for way in range(2):
            stats[2 + way] = upright(stat_recv[way, 1, t * pairs : (t + 1) * pairs])
        lax.fori_loop(t * (pairs // 2), (t + 1) * (pairs // 2), functools.partial(finish, t), 0)
    results[2].start()
    results[3].start()
    reduce_step(len(reduces) - 1)

    @pl.when(place < n - 1)
    def _():
        for copy in to_up:
            copy.wait_send()

    @pl.when(place > 0)
    def _():
        for copy in to_down:
            copy.wait_send()

    if structured:
        for way in range(2):

            @pl.when(turns[way])
            def _():
                onward[way].wait_send()

    for copy in sends_g + sends_u + sends_b + sends_p + [c for group in reduces for c in group]:
        copy.wait_send()

    for way in range(2):

        @pl.when(has[way])
        def _():
            for kind in range(6):
                beside_copy(kind, way).wait_send()

    if structured:
        for j in range(2):
            push(place, j, 0, 0, at(me, near), mine[j]).wait_send()

        @pl.when(middle)
        def _():
            for j in range(2):
                push(place, j, 1, 0, at(me, far), mine[j]).wait_send()

        def sent(k, carry):
            for j in range(2):

                @pl.when((k > 0) & middle)
                def _():
                    push(place, j, 0, k, at(me, near)).wait_send()

                push(place, j, 2, k, at(me, near)).wait_send()
            return carry

        lax.fori_loop(0, 4, sent, 0)
    else:

        def sent(d, carry):
            for j in range(2):
                push(place, j, 0, d, at(me, (place + d) % n), mine[j]).wait_send()
            return carry

        lax.fori_loop(1, n, sent, 0)
    for copy in results:
        copy.wait()


def shards(acts, queries, keys, values, grad_out, gain, router, w_in, w_out, routes, tissue):
    tok, width = acts.shape[1:]
    n = lax.axis_size("seq")
    experts = router.shape[1]
    cap = max(2, 5 * tok // (4 * experts))
    cap = -(-cap // 16) * 16
    rows = experts * cap
    frows = w_in.shape[1]
    span = tok + 2 * REACH
    pairs = width // LANES
    lines = (experts + 1) * pairs
    per = max(1, 256 // frows)
    rounds = reduce_rounds(n, experts)
    most = max(len(masks) for masks in rounds)
    groups = 2 if n == 16 else 1
    bf16, f32 = jnp.bfloat16, jnp.float32
    vmem = pl.BlockSpec(memory_space=pltpu.VMEM)
    hbm = pl.BlockSpec(memory_space=pl.ANY)
    big = jax.ShapeDtypeStruct((tok, width), bf16)
    dma = pltpu.SemaphoreType.DMA
    steps = 4 if n == 16 else n
    outs = pl.pallas_call(
        functools.partial(kernel, n, experts, cap, tissue.shape[1], groups),
        out_shape=[big, big, big, big, jax.ShapeDtypeStruct((lines, LANES), f32)],
        in_specs=[hbm] * 5 + [vmem] * 2 + [hbm] * 2 + [vmem, pl.BlockSpec(memory_space=pltpu.SMEM)],
        out_specs=[hbm] * 4 + [vmem],
        scratch_shapes=[pltpu.VMEM((tok, width), bf16)] * 7
        + [pltpu.VMEM((groups, rows, per * frows), f32)] * 2
        + [
            pltpu.VMEM((n, 2, frows, width), bf16),
            pltpu.VMEM((span, width), bf16),
            pltpu.VMEM((span, width), bf16),
            pltpu.VMEM((tok, span), f32),
            pltpu.VMEM((pairs, 2 * tok, span), f32),
            pltpu.VMEM((tok, width), f32),
            pltpu.VMEM((tok, width), f32),
            pltpu.VMEM((experts, cap, width), bf16),
            pltpu.VMEM((groups, experts, cap, width), bf16),
            pltpu.VMEM((experts, cap, width), bf16),
            pltpu.VMEM((groups, experts, cap, width), bf16),
            pltpu.VMEM((groups, rows, width), f32),
            pltpu.VMEM((groups, rows, 1), f32),
            pltpu.VMEM((groups, experts, cap, width), bf16),
            pltpu.VMEM((groups, experts, cap, width), bf16),
            pltpu.VMEM((groups, experts, 8, LANES), f32),
            pltpu.VMEM((groups, experts, 8, LANES), f32),
            pltpu.VMEM((2, tok, width), f32),
            pltpu.VMEM((4, tok, LANES), f32),
            pltpu.VMEM((2, 2 * pairs, tok), f32),
            pltpu.VMEM((2, 2, 2 * pairs, tok), f32),
            pltpu.VMEM((2, tok, tok), f32),
            pltpu.VMEM((2, tok, width), bf16),
            pltpu.VMEM((2, tok, width), bf16),
            pltpu.VMEM((pairs, 4 * tok, tok), f32),
            pltpu.VMEM((tok, width), bf16),
            pltpu.VMEM((len(rounds), lines, LANES), f32),
            pltpu.VMEM((len(rounds), most, lines, LANES), f32),
            dma((7,)),
            dma((4,)),
            dma((2, 2)),
            dma((2, 2)),
            dma((3, steps, 2)),
            dma((n, 2)),
            dma((4, groups * experts)),
            dma((4, groups * experts)),
            dma((6, 2)),
            dma((6, 2)),
            dma((2,)),
            dma((len(rounds), most)),
            dma((len(rounds), most)),
        ],
        compiler_params=pltpu.CompilerParams(
            collective_id=0, has_side_effects=True, vmem_limit_bytes=60 * 1024 * 1024
        ),
    )(
        acts[0], queries[0], keys[0], values[0], grad_out[0], gain[None], router.T,
        w_in[0], w_out[0], routes[:, :, 0], tissue,
    )
    outs = pl.pallas_call(
        hand_out,
        out_shape=[
            big, big, big, big,
            jax.ShapeDtypeStruct((experts, width), f32), jax.ShapeDtypeStruct((1, width), f32),
        ],
        in_specs=[vmem] * 5,
        out_specs=[vmem] * 6,
    )(*outs)
    return tuple(out[None] for out in outs[:4]) + (outs[4].T, outs[5][0])


def hand_out(*refs):
    for source, target in zip(refs[:4], refs[5:9]):
        target[...] = source[...]
    small, experts = refs[4], refs[9].shape[0]
    pairs = small.shape[0] // (experts + 1)
    for row in range(experts + 1):
        target, line = (refs[9], row) if row < experts else (refs[10], 0)
        for c in range(pairs):
            where = row * pairs + c
            target[line : line + 1, c * LANES : (c + 1) * LANES] = small[where : where + 1, :]


def solution(mesh):
    tiles = P("expert", "seq", None)
    in_specs = (tiles,) * 5 + (P(), P()) + (tiles,) * 3 + (P("expert", None),)
    out_specs = (tiles,) * 4 + (P(), P())
    return jax.shard_map(shards, mesh=mesh, in_specs=in_specs, out_specs=out_specs, check_vma=False)
```

```python
import functools

import jax
import jax.numpy as jnp
from jax import lax
from jax.experimental import pallas as pl
from jax.experimental.pallas import tpu as pltpu
from jax.sharding import PartitionSpec as P

HEAD = 64
REACH = 128
BLOCK = 512
EPS = 1e-06
LANES = 128
NEG = -1e30
GELU_C = 0.7978845608028654
GELU_A = 0.044715
MESH = pl.DeviceIdType.MESH


def dot(a, b, contract, precision=None):
    return lax.dot_general(
        a, b, (contract, ((), ())), preferred_element_type=jnp.float32, precision=precision
    )


def flip(index, mask):
    size = 1
    while size <= mask:
        if mask & size:
            index = index + size - 2 * size * ((index // size) % 2)
        size *= 2
    return index


def reduce_rounds(n, experts):
    bits = [(1 << b, 0) for b in range((experts - 1).bit_length())]
    bits += [(0, 1 << b) for b in range((n - 1).bit_length())]
    rounds = []
    for start in range(0, len(bits), 3):
        masks = [(0, 0)]
        for e, m in bits[start : start + 3]:
            masks += [(a + e, b + m) for a, b in masks]
        rounds.append(masks[1:])
    return rounds


def kernel(
    n, experts, cap, nblocks, groups,
    acts_h, queries_h, keys, values, grad_out_h, gain, router, w_in, w_out, routes, tissue,
    grad_acts_h, grad_q_h, grad_k_h, grad_v_h, small_out,
    acts, queries, grad_out, grad_acts, grad_q, grad_k, grad_v, act_s, slope_s,
    weights, kx, vx, bias, probs, attn, normed_s, u_send, u_slots, g_send, g_slots,
    inner_acc, pick_acc, b_send, b_slots, p_send, p_slots, own_kv,
    stats, stat_send, stat_recv, side_bias, side_q, side_o, side_probs, relay_v, red_send, red_recv,
    local_sem, out_sem, halo_ss, halo_rs, w_ss, w_rs, ex_ss, ex_rs, nb_ss, nb_rs, relay_sem, red_ss, red_rs,
):
    tok, width = acts_h.shape
    span = tok + 2 * REACH
    frows = w_in.shape[0]
    rows = experts * cap
    pairs = width // LANES
    place = lax.axis_index("seq")
    me = lax.axis_index("expert")
    structured = n == 16
    bf16, f32 = jnp.bfloat16, jnp.float32

    def at(expert, seq):
        return (expert, seq)

    def remote(src, dst, ss, rs, where):
        return pltpu.make_async_remote_copy(
            src_ref=src, dst_ref=dst, send_sem=ss, recv_sem=rs, device_id=where, device_id_type=MESH
        )

    barrier = pltpu.get_barrier_semaphore()
    rounds = reduce_rounds(n, experts)
    peers = [at(flip(me, e), flip(place, m)) for masks in rounds for e, m in masks]
    if structured:
        z = place // 4
        peers += [at(me, (place + d) % n) for d in (1, n - 1, 3, n - 3)]
    else:
        peers += [at(me, (place + d) % n) for d in range(1, n)]
        peers += [at((me + d) % experts, place) for d in range(1, experts)]
    for peer in peers:
        pl.semaphore_signal(barrier, inc=1, device_id=peer, device_id_type=MESH)

    own_copies = [
        pltpu.make_async_copy(w_in, weights.at[place, 0], local_sem.at[0]),
        pltpu.make_async_copy(w_out, weights.at[place, 1], local_sem.at[1]),
        pltpu.make_async_copy(keys, kx.at[pl.ds(REACH, tok)], local_sem.at[2]),
        pltpu.make_async_copy(values, vx.at[pl.ds(REACH, tok)], local_sem.at[3]),
        pltpu.make_async_copy(grad_out_h, grad_out, local_sem.at[4]),
        pltpu.make_async_copy(queries_h, queries, local_sem.at[5]),
        pltpu.make_async_copy(acts_h, acts, local_sem.at[6]),
    ]
    for copy in own_copies:
        copy.start()
    lane = lax.broadcasted_iota(jnp.int32, (tok, LANES), 1)
    row_at = lax.broadcasted_iota(jnp.int32, (tok, tok), 0)
    col_at = lax.broadcasted_iota(jnp.int32, (tok, tok), 1)
    spread_routes = jnp.where(row_at == col_at, jnp.broadcast_to(routes[...], (tok, tok)), 0)
    route = jnp.sum(spread_routes.astype(f32), -1, keepdims=True).astype(jnp.int32)
    onehot = (route == lane).astype(f32)
    lower = (row_at > col_at).astype(bf16)
    before = dot(lower, onehot.astype(bf16), ((1,), (0,)))
    rank = jnp.sum(before * onehot, -1, keepdims=True).astype(jnp.int32)
    slot = route * cap + rank
    disp = (slot == lax.broadcasted_iota(jnp.int32, (tok, rows), 1)).astype(bf16)

    here = (place // 2) % 2 if structured else 0
    q_at = place * tok + lax.broadcasted_iota(jnp.int32, (tok, span), 0)
    k_at = place * tok - REACH + lax.broadcasted_iota(jnp.int32, (tok, span), 1)
    live = jnp.zeros((tok, span), jnp.int32)
    for b in range(nblocks):
        live = jnp.where((k_at >= b * BLOCK) & (k_at < (b + 1) * BLOCK), tissue[0, b], live)
    near_by = jnp.abs(q_at - k_at) <= REACH
    allow = near_by & (k_at >= 0) & (k_at < n * tok) & ((live == 1) | (q_at == k_at))
    bias[...] = jnp.where(allow, 0.0, NEG).astype(f32)
    live_own = live[:, REACH : REACH + tok] == 1
    for r, near_side in enumerate(((col_at <= row_at) & (place > 0), (row_at <= col_at) & (place < n - 1))):
        side_bias[r] = jnp.where(near_side & live_own, 0.0, NEG).astype(f32)
    own_copies[4].wait()
    moved_g = dot(disp, grad_out[...], ((0,), (0,))).astype(bf16)
    g_send[...] = moved_g.reshape(experts, cap, width)
    g_slots[here, me] = g_send[me]
    pl.semaphore_wait(barrier, len(peers))

    up, down = at(me, (place + 1) % n), at(me, (place + n - 1) % n)
    to_up = [
        remote(src, dst.at[pl.ds(0, REACH)], halo_ss.at[i, 0], halo_rs.at[i, 0], up)
        for i, (src, dst) in enumerate(((keys, kx), (values, vx)))
    ]
    to_down = [
        remote(src, dst.at[pl.ds(REACH + tok, REACH)], halo_ss.at[i, 1], halo_rs.at[i, 1], down)
        for i, (src, dst) in enumerate(((keys, kx), (values, vx)))
    ]

    heads = 2 * pairs
    targets = (up, down)
    has = (place < n - 1, place > 0)
    comes = (place > 0, place < n - 1)

    def half_rows(t):
        return pl.ds(t * pairs, pairs)

    def half_cols(t):
        return pl.ds(t * (width // 2), width // 2)

    def beside_copy(kind, way):
        if kind == 0:
            src, dst = queries_h, side_q.at[way]
        elif kind == 1:
            src, dst = stat_send.at[0], stat_recv.at[way, 0]
        elif kind < 4:
            src, dst = (stat_send.at[1, half_rows(kind - 2)], stat_recv.at[way, 1, half_rows(kind - 2)])
        else:
            src, dst = grad_acts.at[:, half_cols(kind - 4)], side_o.at[way, :, half_cols(kind - 4)]
        return remote(src, dst, nb_ss.at[kind, way], nb_rs.at[kind, way], targets[way])

    def tell(kinds, ways=(0, 1)):
        for way in ways:

            @pl.when(has[way])
            def _():
                for kind in kinds:
                    beside_copy(kind, way).start()

    def hear(kinds):
        for way in range(2):

            @pl.when(comes[way])
            def _():
                for kind in kinds:
                    beside_copy(kind, way).wait_recv()

    if structured:
        seat = place % 4
        over = (
            remote(values, relay_v, halo_ss.at[1, 0], relay_sem.at[0], at(me, (place + n - 2) % n)),
            remote(values, relay_v, halo_ss.at[1, 1], relay_sem.at[0], at(me, (place + 2) % n)),
        )
        onward = (
            remote(relay_v, vx.at[pl.ds(0, REACH)], relay_sem.at[1], halo_rs.at[1, 0], at(me, (place + 3) % n)),
            remote(
                relay_v, vx.at[pl.ds(REACH + tok, REACH)], relay_sem.at[1], halo_rs.at[1, 1], at(me, (place + n - 3) % n)
            ),
        )
        turns = ((seat == 1) & (place < n - 3), (seat == 2) & (place > 2))
        aside = (seat == 3, seat == 0)
    else:
        aside = (False, False)

    for way, copies in enumerate((to_up, to_down)):

        @pl.when(has[way])
        def _():
            copies[0].start()

        @pl.when(has[way] & jnp.logical_not(aside[way]))
        def _():
            copies[1].start()

        if structured:

            @pl.when(has[way] & aside[way])
            def _():
                over[way].start()

    def push(owner, j, kind, step, where, src=None):
        return remote(
            weights.at[owner, j] if src is None else src,
            weights.at[owner, j],
            w_ss.at[kind, step, j],
            w_rs.at[owner, j],
            where,
        )

    def landed(owner, j):
        push(owner, j, 0, 0, up).wait_recv()

    mine = (w_in, w_out)
    if structured:
        x = (place // 2) % 2
        low = place % 4
        middle = (z == 1) | (z == 2)
        near, far = flip(place, 4), flip(place, 12)
        other_c = flip(place, 1)

        def column(k):
            return jnp.where(
                k == 0, z, jnp.where(k == 1, z + 1 - 2 * (z % 2), jnp.where(k == 2, 2 - z // 2, 3 - 3 * (z // 2)))
            )

        for j in range(2):
            push(place, j, 0, 0, at(me, near), mine[j]).start()

        @pl.when(middle)
        def _():
            for j in range(2):
                push(place, j, 1, 0, at(me, far), mine[j]).start()

        for j in range(2):
            push(place, j, 2, 0, at(me, other_c), mine[j]).start()
    else:

        def spread(d, carry):
            for j in range(2):
                push(place, j, 0, d, at(me, (place + d) % n), mine[j]).start()
            return carry

        lax.fori_loop(1, n, spread, 0)

    offsets = [(dx, d) for dx in range(groups) for d in range(experts)][1:]

    def beside(dx, d):
        return at((me + d) % experts, flip(place, 2 * dx))

    def exchange(piece, slots, which):
        return [
            remote(
                piece(here + dx * (1 - 2 * here), (me + d) % experts),
                slots.at[here, me],
                ex_ss.at[which, dx * experts + d],
                ex_rs.at[which, here * experts + me],
                beside(dx, d),
            )
            for dx, d in offsets
        ]

    def arrivals(slots, which):
        for dx, d in offsets:
            group, source = here + dx * (1 - 2 * here), (me + d) % experts
            remote(
                slots.at[group, source],
                slots.at[group, source],
                ex_ss.at[which, dx * experts + d],
                ex_rs.at[which, group * experts + source],
                beside(dx, d),
            ).wait_recv()

    half = lax.broadcasted_iota(jnp.int32, (tok, LANES), 1) < HEAD
    first = half.astype(bf16)
    second = (1.0 - half.astype(f32)).astype(bf16)

    def stack(value):
        return jnp.concatenate([value * first, value * second], 0)

    own_copies[2].wait()
    own_copies[3].wait()
    if structured:
        for way in range(2):

            @pl.when(turns[way])
            def _():
                over[way].wait_recv()
                onward[way].start()

    @pl.when(place > 0)
    def _():
        for copy in to_up:
            copy.wait_recv()

    for way in range(2):

        @pl.when(jnp.logical_not(comes[way]))
        def _():
            side_q[way] = jnp.zeros((tok, width), bf16)
            side_o[way] = jnp.zeros((tok, width), bf16)
            stat_recv[way] = jnp.zeros((2, heads, tok), f32)

    @pl.when(place == 0)
    def _():
        kx[pl.ds(0, REACH), :] = jnp.zeros((REACH, width), bf16)
        vx[pl.ds(0, REACH), :] = jnp.zeros((REACH, width), bf16)

    @pl.when(place < n - 1)
    def _():
        for copy in to_down:
            copy.wait_recv()

    @pl.when(place == n - 1)
    def _():
        kx[pl.ds(REACH + tok, REACH), :] = jnp.zeros((REACH, width), bf16)
        vx[pl.ds(REACH + tok, REACH), :] = jnp.zeros((REACH, width), bf16)

    sends_g = exchange(lambda group, expert: g_send.at[expert], g_slots, 0)
    for copy in sends_g:
        copy.start()
    own_copies[5].wait()

    if structured:

        def relay(k):
            owner = column(k) * 4 + low
            for j in range(2):
                landed(owner, j)

                @pl.when(middle)
                def _():
                    push(owner, j, 0, k, at(me, jnp.where(k == 1, far, near))).start()

                push(owner, j, 2, k, at(me, other_c)).start()

        relay(1)

        @pl.when(middle)
        def _():
            relay(2)

    def keep(kind, i, line):
        stats[kind] = jnp.where(
            lane == 2 * i, line[:tok], jnp.where(lane == 2 * i + 1, line[tok:], stats[kind])
        )

    def forward(i, carry):
        cols = pl.ds(pl.multiple_of(i * LANES, LANES), LANES)
        scores = dot(stack(queries[:, cols]), kx[:, cols], ((1,), (1,))) * HEAD ** (-0.5)
        both = jnp.concatenate([bias[...], bias[...]], 0)
        scores = scores + both
        top = jnp.max(scores, -1, keepdims=True)
        weight = jnp.exp(scores - top)
        total = jnp.sum(weight, -1, keepdims=True)
        prob = weight / total
        probs[i] = prob
        keep(0, i, top + jnp.log(total))
        mixed = dot(prob.astype(bf16), vx[:, cols], ((1,), (0,)))
        attn[:, cols] = jnp.where(half, mixed[:tok], mixed[tok:])
        return carry

    stats[...] = jnp.zeros_like(stats)
    lax.fori_loop(0, pairs, forward, 0)
    stat_send[0] = jnp.transpose(stats[0])[:heads]

    own_copies[6].wait()
    mid = acts[...].astype(f32) + attn[...]
    rms = lax.rsqrt(jnp.mean(mid * mid, -1, keepdims=True) + EPS)
    normed_s[...] = mid * rms
    inner = (normed_s[...] * gain[...]).astype(bf16)
    moved_u = dot(disp, inner, ((0,), (0,))).astype(bf16)
    u_send[...] = moved_u.reshape(experts, cap, width)
    u_slots[here, me] = u_send[me]
    sends_u = exchange(lambda group, expert: u_send.at[expert], u_slots, 1)
    for copy in sends_u:
        copy.start()
    late = (place == n - 5, place == 4) if structured else (False, False)
    tell((1,))
    for way in range(2):

        @pl.when(has[way] & jnp.logical_not(late[way]))
        def _():
            beside_copy(0, way).start()


    inner_f = inner.astype(f32)
    router_f = router[...].astype(f32)
    r_lane = lane
    logits = jnp.full((tok, LANES), NEG, f32)
    for e in range(experts):
        logits = jnp.where(lane == e, jnp.sum(inner_f * router_f[e : e + 1, :], -1, keepdims=True), logits)
    chance = jnp.exp(logits - jnp.max(logits, -1, keepdims=True))
    chance = chance / jnp.sum(chance, -1, keepdims=True)
    chosen = (route == r_lane).astype(f32)
    pick = jnp.sum(chance * chosen, -1, keepdims=True)

    own_copies[0].wait()
    own_copies[1].wait()
    inner_acc[...] = jnp.zeros_like(inner_acc)
    pick_acc[...] = jnp.zeros_like(pick_acc)
    per = max(1, 256 // frows)

    span_w = per * frows

    def first_half(start):
        wi = weights[pl.ds(start, per), 0].reshape(span_w, width)
        hidden = dot(u_slots[...].reshape(groups * rows, width), wi, ((1,), (1,)))
        square = hidden * hidden
        t = jnp.tanh(GELU_C * hidden * (1.0 + GELU_A * square))
        gate = 0.5 * (1.0 + t)
        act = (hidden * gate).astype(bf16).astype(f32)
        slope = gate + 0.5 * hidden * (1.0 - t * t) * (GELU_C * (1.0 + 3.0 * GELU_A * square))
        act_s[...] = act.reshape(groups, rows, span_w)
        slope_s[...] = slope.reshape(groups, rows, span_w)

    def second_half(start):
        wi = weights[pl.ds(start, per), 0].reshape(span_w, width)
        wo = weights[pl.ds(start, per), 1].reshape(span_w, width)
        back = dot(g_slots[...].reshape(groups * rows, width), wo, ((1,), (1,)))
        act = act_s[...].reshape(groups * rows, span_w)
        slope = slope_s[...].reshape(groups * rows, span_w)
        pick_acc[...] += jnp.sum(act * back, -1, keepdims=True).reshape(groups, rows, 1)
        inner_acc[...] += dot((back * slope).astype(bf16), wi, ((1,), (0,))).reshape(groups, rows, width)

    eye = (
        lax.broadcasted_iota(jnp.int32, (cap, LANES), 0) == lax.broadcasted_iota(jnp.int32, (cap, LANES), 1)
    ).astype(f32)

    def last_half(start, group):
        wi = weights[pl.ds(start, per), 0].reshape(span_w, width)
        wo = weights[pl.ds(start, per), 1].reshape(span_w, width)
        back = dot(g_slots[group].reshape(rows, width), wo, ((1,), (1,)))
        picked = pick_acc[group] + jnp.sum(act_s[group] * back, -1, keepdims=True)
        total = inner_acc[group] + dot((back * slope_s[group]).astype(bf16), wi, ((1,), (0,)))
        b_send[group] = total.astype(bf16).reshape(experts, cap, width)
        for e in range(experts):
            line = jnp.sum(picked[e * cap : (e + 1) * cap] * eye, 0, keepdims=True)
            p_send[group, e] = jnp.broadcast_to(line, (8, LANES))

    sends_b = exchange(lambda group, expert: b_send.at[group, expert], b_slots, 2)
    sends_p = exchange(lambda group, expert: p_send.at[group, expert], p_slots, 3)

    def give_back(wanted):
        for (dx, d), p_copy, b_copy in list(zip(offsets, sends_p, sends_b))[::-1]:
            if dx in wanted:
                p_copy.start()
                b_copy.start()

    if structured:

        @pl.when(middle)
        def _():
            relay(3)

        @pl.when(jnp.logical_not(middle))
        def _():
            relay(2)

        arrivals(g_slots, 0)
        arrivals(u_slots, 1)

        def step(k, carry):
            start = column(k) * 4 + x * 2
            landed(start + 1 - place % 2, 0)
            first_half(start)
            landed(start + 1 - place % 2, 1)
            second_half(start)
            return carry

        lax.fori_loop(0, 3, step, 0)

        @pl.when(jnp.logical_not(middle))
        def _():
            relay(3)

        start = column(3) * 4 + x * 2
        landed(start + 1 - place % 2, 0)
        first_half(start)
        landed(start + 1 - place % 2, 1)
    else:

        def settle(d, carry):
            for j in range(2):
                landed((place + d) % n, j)
            return carry

        lax.fori_loop(1, n, settle, 0)
        arrivals(g_slots, 0)
        arrivals(u_slots, 1)

        def step(j, carry):
            first_half(j * per)
            second_half(j * per)
            return carry

        lax.fori_loop(0, n // per - 1, step, 0)
        start = n - per
        first_half(start)

    for dx in range(groups)[::-1]:
        last_half(start, here + dx * (1 - 2 * here))
        give_back((dx,))

    for way in range(2):

        @pl.when(has[way] & late[way])
        def _():
            beside_copy(0, way).start()

    hear((0, 1))

    def column_of(table, at_lane):
        return jnp.sum(jnp.where(lane == at_lane, table, 0.0), -1, keepdims=True)

    def upright(table):
        if table.shape[0] < tok:
            table = jnp.concatenate([table, jnp.zeros((tok - table.shape[0], tok), f32)], 0)
        return jnp.transpose(table)

    for way in range(2):
        stats[2 + way] = upright(stat_recv[way, 0])
    own = pl.ds(REACH, tok)

    def beside_probs(i, carry):
        cols = pl.ds(pl.multiple_of(i * LANES, LANES), LANES)
        for way in range(2):
            scores = dot(stack(side_q[way, :, cols]), kx[own, cols], ((1,), (1,))) * HEAD ** (-0.5)
            scores = scores + jnp.concatenate([side_bias[way], side_bias[way]], 0)
            line = jnp.concatenate([column_of(stats[2 + way], 2 * i), column_of(stats[2 + way], 2 * i + 1)], 0)
            side_probs[i, way * 2 * tok : (way + 1) * 2 * tok, :] = jnp.exp(scores - line)
        return carry

    lax.fori_loop(0, pairs, beside_probs, 0)

    b_slots[here, me] = b_send[here, me]
    p_slots[here, me] = p_send[here, me]
    arrivals(p_slots, 3)
    arrivals(b_slots, 2)

    normed = normed_s[...]
    part_inner = dot(disp, b_slots[0].reshape(rows, width), ((1,), (0,)))
    for group in range(1, groups):
        part_inner = part_inner + dot(disp, b_slots[group].reshape(rows, width), ((1,), (0,)))
    picks = jnp.zeros((tok, LANES), f32)
    for e in range(experts):
        line = p_slots[0, e, :1, :]
        for group in range(1, groups):
            line = line + p_slots[group, e, :1, :]
        picks = jnp.where(route == e, line, picks)
    grad_pick = jnp.sum(jnp.where(rank == lane, picks, 0.0), -1, keepdims=True)
    grad_logits = (grad_pick * pick) * (chosen - chance)
    grad_inner = pick * part_inner

    def pack(at_row, line):
        for c in range(pairs):
            where = at_row * pairs + c
            red_send[0, where : where + 1, :] = line[:, c * LANES : (c + 1) * LANES]

    inner_f = (normed * gain[...]).astype(bf16).astype(f32)
    for e in range(experts):
        column_e = grad_logits[:, e : e + 1]
        grad_inner = grad_inner + column_e * router_f[e : e + 1, :]
        pack(e, jnp.sum(inner_f * column_e, 0, keepdims=True))
    pack(experts, jnp.sum(grad_inner * normed, 0, keepdims=True))
    grad_normed = grad_inner * gain[...]
    grad_mid = rms * (
        grad_normed - normed * jnp.mean(grad_normed * normed, -1, keepdims=True)
    ) + grad_out[...].astype(f32)
    grad_acts[...] = grad_mid.astype(bf16)
    results = [
        pltpu.make_async_copy(source, target, out_sem.at[i])
        for i, (source, target) in enumerate(
            ((grad_acts, grad_acts_h), (grad_q, grad_q_h), (grad_k, grad_k_h), (grad_v, grad_v_h))
        )
    ]
    reduces = [
        [
            remote(red_send.at[j], red_recv.at[j, i], red_ss.at[j, i], red_rs.at[j, i], at(flip(me, e), flip(place, m)))
            for i, (e, m) in enumerate(masks)
        ]
        for j, masks in enumerate(rounds)
    ]
    for copy in reduces[0]:
        copy.start()
    results[0].start()
    tell((4,))

    def reduce_step(j):
        total = red_send[j]
        for i, copy in enumerate(reduces[j]):
            copy.wait_recv()
            total = total + red_recv[j, i]
        if j + 1 < len(reduces):
            red_send[j + 1] = total
            for copy in reduces[j + 1]:
                copy.start()
        else:
            small_out[...] = total


    def backward(i, carry):
        cols = pl.ds(pl.multiple_of(i * LANES, LANES), LANES)
        o_stack = stack(grad_acts[:, cols])
        q_stack = stack(queries[:, cols])
        prob = probs[i]
        grad_probs = dot(o_stack, vx[:, cols], ((1,), (1,)))
        own_value = dot(prob[:, REACH : REACH + tok].astype(bf16), o_stack, ((0,), (0,)))
        delta = jnp.sum(prob * grad_probs, -1, keepdims=True)
        keep(1, i, delta)
        grad_scores = (prob * (grad_probs - delta) * HEAD ** (-0.5)).astype(bf16)
        query_terms = dot(grad_scores, kx[:, cols], ((1,), (0,)))
        grad_q[:, cols] = jnp.where(half, query_terms[:tok], query_terms[tok:]).astype(bf16)
        own_key = dot(grad_scores[:, REACH : REACH + tok], q_stack, ((0,), (0,)))
        own_kv[0, :, cols] = own_key
        own_kv[1, :, cols] = own_value
        return carry

    for t in range(2):
        lax.fori_loop(t * (pairs // 2), (t + 1) * (pairs // 2), backward, 0)
        stat_send[1, half_rows(t)] = jnp.transpose(stats[1])[t * pairs : (t + 1) * pairs]
        tell((2, 5) if t == 0 else (3,))
    results[1].start()
    for j in range(len(reduces) - 1):
        reduce_step(j)

    def finish(t, i, carry):
        cols = pl.ds(pl.multiple_of(i * LANES, LANES), LANES)
        o_all = jnp.concatenate([stack(side_o[way, :, cols]) for way in range(2)], 0)
        q_all = jnp.concatenate([stack(side_q[way, :, cols]) for way in range(2)], 0)
        prob = side_probs[i]
        line = jnp.concatenate(
            [column_of(stats[2 + way], 2 * i + h - t * pairs) for way in range(2) for h in range(2)], 0
        )
        grad_probs = dot(o_all, vx[own, cols], ((1,), (1,)))
        grad_scores = (prob * (grad_probs - line) * HEAD ** (-0.5)).astype(bf16)
        grad_k[:, cols] = (own_kv[0, :, cols] + dot(grad_scores, q_all, ((0,), (0,)))).astype(bf16)
        grad_v[:, cols] = (own_kv[1, :, cols] + dot(prob.astype(bf16), o_all, ((0,), (0,)))).astype(bf16)
        return carry

    for t in range(2):
        hear((2 + t, 4 + t))
        for way in range(2):
            stats[2 + way] = upright(stat_recv[way, 1, t * pairs : (t + 1) * pairs])
        lax.fori_loop(t * (pairs // 2), (t + 1) * (pairs // 2), functools.partial(finish, t), 0)
    results[2].start()
    results[3].start()
    reduce_step(len(reduces) - 1)

    @pl.when(place < n - 1)
    def _():
        for copy in to_up:
            copy.wait_send()

    @pl.when(place > 0)
    def _():
        for copy in to_down:
            copy.wait_send()

    if structured:
        for way in range(2):

            @pl.when(turns[way])
            def _():
                onward[way].wait_send()

    for copy in sends_g + sends_u + sends_b + sends_p + [c for group in reduces for c in group]:
        copy.wait_send()

    for way in range(2):

        @pl.when(has[way])
        def _():
            for kind in range(6):
                beside_copy(kind, way).wait_send()

    if structured:
        for j in range(2):
            push(place, j, 0, 0, at(me, near), mine[j]).wait_send()

        @pl.when(middle)
        def _():
            for j in range(2):
                push(place, j, 1, 0, at(me, far), mine[j]).wait_send()

        def sent(k, carry):
            for j in range(2):

                @pl.when((k > 0) & middle)
                def _():
                    push(place, j, 0, k, at(me, near)).wait_send()

                push(place, j, 2, k, at(me, near)).wait_send()
            return carry

        lax.fori_loop(0, 4, sent, 0)
    else:

        def sent(d, carry):
            for j in range(2):
                push(place, j, 0, d, at(me, (place + d) % n), mine[j]).wait_send()
            return carry

        lax.fori_loop(1, n, sent, 0)
    for copy in results:
        copy.wait()


def shards(acts, queries, keys, values, grad_out, gain, router, w_in, w_out, routes, tissue):
    tok, width = acts.shape[1:]
    n = lax.axis_size("seq")
    experts = router.shape[1]
    cap = max(2, 5 * tok // (4 * experts))
    cap = -(-cap // 16) * 16
    rows = experts * cap
    frows = w_in.shape[1]
    span = tok + 2 * REACH
    pairs = width // LANES
    lines = (experts + 1) * pairs
    per = max(1, 256 // frows)
    rounds = reduce_rounds(n, experts)
    most = max(len(masks) for masks in rounds)
    groups = 2 if n == 16 else 1
    bf16, f32 = jnp.bfloat16, jnp.float32
    vmem = pl.BlockSpec(memory_space=pltpu.VMEM)
    hbm = pl.BlockSpec(memory_space=pl.ANY)
    big = jax.ShapeDtypeStruct((tok, width), bf16)
    dma = pltpu.SemaphoreType.DMA
    steps = 4 if n == 16 else n
    outs = pl.pallas_call(
        functools.partial(kernel, n, experts, cap, tissue.shape[1], groups),
        out_shape=[big, big, big, big, jax.ShapeDtypeStruct((lines, LANES), f32)],
        in_specs=[hbm] * 5 + [vmem] * 2 + [hbm] * 2 + [vmem, pl.BlockSpec(memory_space=pltpu.SMEM)],
        out_specs=[hbm] * 4 + [vmem],
        scratch_shapes=[pltpu.VMEM((tok, width), bf16)] * 7
        + [pltpu.VMEM((groups, rows, per * frows), f32)] * 2
        + [
            pltpu.VMEM((n, 2, frows, width), bf16),
            pltpu.VMEM((span, width), bf16),
            pltpu.VMEM((span, width), bf16),
            pltpu.VMEM((tok, span), f32),
            pltpu.VMEM((pairs, 2 * tok, span), f32),
            pltpu.VMEM((tok, width), f32),
            pltpu.VMEM((tok, width), f32),
            pltpu.VMEM((experts, cap, width), bf16),
            pltpu.VMEM((groups, experts, cap, width), bf16),
            pltpu.VMEM((experts, cap, width), bf16),
            pltpu.VMEM((groups, experts, cap, width), bf16),
            pltpu.VMEM((groups, rows, width), f32),
            pltpu.VMEM((groups, rows, 1), f32),
            pltpu.VMEM((groups, experts, cap, width), bf16),
            pltpu.VMEM((groups, experts, cap, width), bf16),
            pltpu.VMEM((groups, experts, 8, LANES), f32),
            pltpu.VMEM((groups, experts, 8, LANES), f32),
            pltpu.VMEM((2, tok, width), f32),
            pltpu.VMEM((4, tok, LANES), f32),
            pltpu.VMEM((2, 2 * pairs, tok), f32),
            pltpu.VMEM((2, 2, 2 * pairs, tok), f32),
            pltpu.VMEM((2, tok, tok), f32),
            pltpu.VMEM((2, tok, width), bf16),
            pltpu.VMEM((2, tok, width), bf16),
            pltpu.VMEM((pairs, 4 * tok, tok), f32),
            pltpu.VMEM((tok, width), bf16),
            pltpu.VMEM((len(rounds), lines, LANES), f32),
            pltpu.VMEM((len(rounds), most, lines, LANES), f32),
            dma((7,)),
            dma((4,)),
            dma((2, 2)),
            dma((2, 2)),
            dma((3, steps, 2)),
            dma((n, 2)),
            dma((4, groups * experts)),
            dma((4, groups * experts)),
            dma((6, 2)),
            dma((6, 2)),
            dma((2,)),
            dma((len(rounds), most)),
            dma((len(rounds), most)),
        ],
        compiler_params=pltpu.CompilerParams(
            collective_id=0, has_side_effects=True, vmem_limit_bytes=60 * 1024 * 1024
        ),
    )(
        acts[0], queries[0], keys[0], values[0], grad_out[0], gain[None], router.T,
        w_in[0], w_out[0], routes[:, :, 0], tissue,
    )
    outs = pl.pallas_call(
        hand_out,
        out_shape=[
            big, big, big, big,
            jax.ShapeDtypeStruct((experts, width), f32), jax.ShapeDtypeStruct((1, width), f32),
        ],
        in_specs=[vmem] * 5,
        out_specs=[vmem] * 6,
    )(*outs)
    return tuple(out[None] for out in outs[:4]) + (outs[4].T, outs[5][0])


def hand_out(*refs):
    for source, target in zip(refs[:4], refs[5:9]):
        target[...] = source[...]
    small, experts = refs[4], refs[9].shape[0]
    pairs = small.shape[0] // (experts + 1)
    for row in range(experts + 1):
        target, line = (refs[9], row) if row < experts else (refs[10], 0)
        for c in range(pairs):
            where = row * pairs + c
            target[line : line + 1, c * LANES : (c + 1) * LANES] = small[where : where + 1, :]


def solution(mesh):
    tiles = P("expert", "seq", None)
    in_specs = (tiles,) * 5 + (P(), P()) + (tiles,) * 3 + (P("expert", None),)
    out_specs = (tiles,) * 4 + (P(), P())
    return jax.shard_map(shards, mesh=mesh, in_specs=in_specs, out_specs=out_specs, check_vma=False)
```
